256 devices in a mesh: pair: 64 (over y, z, core), aux: 4 (over x).
Axes of the slice: x: 4, y: 4, z: 8, core: 2. Of those that a mesh axis runs over, the one named last changes fastest.
Arguments:
- factors: bfloat16 [64, 8192, 8, 128], P('pair', 'aux'), may hold values from -0.0625 to 0.0625
- amplitudes: bfloat16 [3072, 128, 128], P('pair'), may hold values from -6 to 6
- block_list: int32 [3072, 3], P('pair'), may hold values from 0 to 63, as said below
- owner_map: int32 [64], replicated, may hold values from 0 to 63, as said below
Outputs:
- residual_blocks: bfloat16 [3072, 128, 128], P('pair')
The draws below stay inside these ranges and needn't reach their ends.
Inputs may be any that keep to these rules, and one draw needn't show every extreme that they name: `block_list`: each row (k, A, C) names an occupied orbital below 64 and two virtual blocks below 8; no row repeats. Among the 48 rows of one device at most 2 have orbitals with the same owner_map entry, and exactly 2 for some entry on every device. `owner_map`: A permutation: entry k is the row of factors that holds orbital k.
All inputs are finite; a program needn't handle non-finite values.
Results may differ from the reference program's by a relative error of at most 0.0046.
Values may be sent and summed in bfloat16 or wider, within the bound.
A program may use at most 64 MiB of HBM per device.

```python
import jax
import jax.numpy as jnp
from jax import lax

VB = 128
NV = 8
NAUX = 8192
NO = 64
BLK_DEV = 48
NBLK = 3072
N_PAIR = 64


def common_layout(key):
    return jax.random.permutation(jax.random.fold_in(key, 11), NO).astype(jnp.int32)


def draw_owner_map(key, part):
    return common_layout(key)


def draw_block_list(key, part):
    owner_table = common_layout(key)
    orbital_at = jnp.argsort(owner_table).astype(jnp.int32)
    senders = jnp.arange(N_PAIR, dtype=jnp.int32)
    distances = jnp.arange(N_PAIR, dtype=jnp.int32)
    scores = jax.random.permutation(jax.random.fold_in(key, 17), N_PAIR).astype(jnp.int32)
    special = (distances == N_PAIR // 2) | (distances == N_PAIR - 1) | (distances == 1)
    priority = scores + jnp.where(special, -2 * N_PAIR, 0)
    reach_set = jnp.argsort(priority)[:BLK_DEV // 2].astype(jnp.int32)
    pick_key = jax.random.fold_in(key, 23)
    chosen = jax.vmap(lambda sender: jax.random.permutation(jax.random.fold_in(pick_key, sender), BLK_DEV))(senders)
    chosen = chosen.astype(jnp.int32)
    ranks = chosen // 2
    offsets = reach_set[ranks]
    owners = (senders[:, None] - offsets) % N_PAIR
    combos = chosen
    table_key = jax.random.fold_in(key, 37)
    tables = jax.vmap(lambda owner: jax.random.permutation(jax.random.fold_in(table_key, owner), NV * NV))(senders)
    tables = tables.astype(jnp.int32)
    codes = tables[owners, combos]
    block_a = codes // NV
    block_c = codes % NV
    orbitals = orbital_at[owners]
    listed = jnp.stack([orbitals, block_a, block_c], axis=-1)
    return listed.reshape(N_PAIR * BLK_DEV, 3).astype(jnp.int32)


def block_levels(stream_key, shape, split, least, high):
    def one(dim, parts):
        heights = jax.random.uniform(jax.random.fold_in(jax.random.fold_in(stream_key, 6), dim), (parts,), jnp.float32, least / len(split), high / len(split))
        return jnp.repeat(jnp.exp(heights), shape[dim] // parts).reshape((-1,) + (1,) * (len(shape) - dim - 1))

    level = one(*split[0])
    for cut in split[1:]:
        level = level * one(*cut)
    return level


def scatter_about(own_key, shape, scale, most, cuts=(), kind=jnp.bfloat16):
    entries = scale * jax.random.normal(own_key, shape, jnp.float32)
    if cuts:
        entries = entries * block_levels(own_key, shape, cuts, -0.22, 0.18)
    return jnp.clip(entries, -most, most).astype(kind)


def setup_inputs(seed: int = 0) -> dict:
    streams_of = jax.random.split(jax.random.key(seed), 5)
    factors = scatter_about(streams_of[0], (NO, NAUX, NV, VB), NAUX ** -0.5, 0.0625, ((0, 64), (1, 4)))
    amplitudes = scatter_about(streams_of[1], (NBLK, VB, VB), ((NAUX * NV / (BLK_DEV * N_PAIR * VB)) ** 0.5), 6.0, ((0, 64),))
    block_list = draw_block_list(jax.random.fold_in(streams_of[4], 71), 0)
    owner_map = draw_owner_map(jax.random.fold_in(streams_of[4], 71), 0)
    return dict(factors=factors, amplitudes=amplitudes, block_list=block_list, owner_map=owner_map)


def reference(factors, amplitudes, block_list, owner_map):
    orbitals = block_list[:, 0].astype(jnp.int32)
    block_a = block_list[:, 1].astype(jnp.int32)
    block_c = block_list[:, 2].astype(jnp.int32)
    rows = owner_map[orbitals].astype(jnp.int32)
    flipped = jnp.transpose(amplitudes.astype(jnp.float32), (0, 2, 1))
    placed = jnp.zeros((NO, NV, VB, NV, VB), jnp.float32).at[rows, block_c, :, block_a, :].add(flipped)
    placed = placed.reshape(NO, NV * VB, NV * VB)
    wide_factors = factors.astype(jnp.float32).reshape(NO, NAUX, NV * VB)

    def accumulate_rows(running, inputs):
        factor_rows, weights = inputs
        return running + jnp.dot(factor_rows, weights, preferred_element_type=jnp.float32), None

    start_total = jnp.zeros((NAUX, NV * VB), jnp.float32)
    summed, unused = lax.scan(accumulate_rows, start_total, (wide_factors, placed))
    inter = summed.astype(jnp.bfloat16).astype(jnp.float32)

    def project_rows(carry, factor_rows):
        return carry, jnp.dot(inter.T, factor_rows, preferred_element_type=jnp.float32)

    unused_carry, projected = lax.scan(project_rows, jnp.zeros((), jnp.float32), wide_factors)
    projected = projected.reshape(NO, NV, VB, NV, VB)
    picked = projected[rows, block_a, :, block_c, :]
    return picked.astype(jnp.bfloat16)
```

```python
import functools

import jax
import jax.numpy as jnp
from jax import lax
from jax.experimental import pallas as pl
from jax.experimental.pallas import tpu as pltpu
from jax.sharding import PartitionSpec as P

CAP = 2
NY = 4
F32 = jnp.float32
BF16 = jnp.bfloat16
MESH = pl.DeviceIdType.MESH
NT = (((1,), (1,)), ((), ()))


def middle_kernel(
    nz, nx, f_ref, w_ref, out_ref, wall, sibtx, sibrx, part, ytx1, yrx1, ytx2, yrx2, ztx, zrx, xt,
    ptx, prx, relay, acc, s_w, r_w, s_sib, r_sib, s_y1, r_y1, s_y2, r_y2, s_z, r_z, s_gz, r_gz,
    s_gy, r_gy, s_gs, r_gs, s_p, r_p,
):
    pair, aux = lax.axis_index("pair"), lax.axis_index("aux")
    core, z, y = lax.rem(pair, 2), lax.rem(pair // 2, nz), pair // (2 * nz)
    half = sibtx.shape[2]
    seg = half // nz
    mid = half // 2
    cols = part.shape[3]
    rows = 2 * half

    def at(y_, z_, c_):
        return {"pair": (lax.rem(y_ + NY, NY) * nz + lax.rem(z_ + nz, nz)) * 2 + c_}

    sib = at(y, z, 1 - core)
    up, down = at(y + 1, z, core), at(y - 1, z, core)
    right, left = {"aux": lax.rem(aux + 1, nx)}, {"aux": lax.rem(aux + nx - 1, nx)}

    def copy(src, dst, send, recv, to):
        return pltpu.make_async_remote_copy(
            src_ref=src, dst_ref=dst, send_sem=send, recv_sem=recv, device_id=to, device_id_type=MESH
        )

    barrier = pltpu.get_barrier_semaphore()
    for peer in (sib, up, down, right, left):
        pl.semaphore_signal(barrier, inc=1, device_id=peer, device_id_type=MESH)

    def greet(d, carry):
        pl.semaphore_signal(barrier, inc=1, device_id=at(y, z + d, core), device_id_type=MESH)
        return carry

    lax.fori_loop(1, nz, greet, 0)
    pl.semaphore_wait(barrier, 5 + nz - 1)

    sent = []

    def go(*args):
        c = copy(*args)
        c.start()
        sent.append(c)
        return c

    go(w_ref, wall.at[0], s_w.at[0], r_w.at[0], right)
    go(w_ref, wall.at[1], s_w.at[1], r_w.at[1], left)

    def landed(dst, recv):
        copy(dst, dst, recv, recv, sib).wait_recv()

    own = pl.multiple_of(core * half, half)
    other = pl.multiple_of((1 - core) * half, half)

    def stage_a(t):
        if t == 1:
            landed(wall.at[0], r_w.at[0])
            go(wall.at[0, :half], wall.at[2, :half], s_w.at[2], r_w.at[2], right)
            landed(wall.at[1], r_w.at[1])
            go(wall.at[1, half:], wall.at[2, half:], s_w.at[3], r_w.at[3], left)
        if t == 3:
            landed(wall.at[2, :half], r_w.at[2])
            landed(wall.at[2, half:], r_w.at[3])
        w = w_ref if t == 0 else wall.at[t - 1]
        w_both = jnp.concatenate([w[pl.ds(other, half), :], w[pl.ds(own, half), :]], axis=0)

        def block(b, carry):
            got = lax.dot_general(
                w_both, f_ref[pl.ds(pl.multiple_of(b * cols, cols), cols), :], NT,
                preferred_element_type=F32,
            )
            sibtx[t, b] = got[:half].astype(BF16)
            part[t, b] = got[half:]
            return carry

        lax.fori_loop(0, NY, block, 0)
        go(sibtx.at[t], sibrx.at[t], s_sib.at[t], r_sib.at[t], sib)

    def stage_b(t):
        landed(sibrx.at[t], r_sib.at[t])

        def block(b, carry):
            part[t, b] = part[t, b] + sibrx[t, b].astype(F32)
            return carry

        lax.fori_loop(0, NY, block, 0)
        ytx1[t] = part[t, lax.rem(y + 2, NY)].astype(BF16)
        go(ytx1.at[t, :mid], yrx1.at[t, 0], s_y1.at[t, 0], r_y1.at[t, 0], up)
        go(ytx1.at[t, mid:], yrx1.at[t, 1], s_y1.at[t, 1], r_y1.at[t, 1], down)

    def stage_c(t):
        above, below = lax.rem(y + 1, NY), lax.rem(y + NY - 1, NY)
        landed(yrx1.at[t, 0], r_y1.at[t, 0])
        ytx2[t, 0, :mid] = (part[t, above, :mid] + yrx1[t, 0].astype(F32)).astype(BF16)
        ytx2[t, 0, mid:] = part[t, above, mid:].astype(BF16)
        go(ytx2.at[t, 0], yrx2.at[t, 0], s_y2.at[t, 0], r_y2.at[t, 0], up)
        landed(yrx1.at[t, 1], r_y1.at[t, 1])
        ytx2[t, 1, :mid] = part[t, below, :mid].astype(BF16)
        ytx2[t, 1, mid:] = (part[t, below, mid:] + yrx1[t, 1].astype(F32)).astype(BF16)
        go(ytx2.at[t, 1], yrx2.at[t, 1], s_y2.at[t, 1], r_y2.at[t, 1], down)

    def z_copy(t, d):
        to = lax.rem(z + d, nz)
        return copy(ztx.at[t, to], zrx.at[t, d], s_z.at[t, d], r_z.at[t, d], at(y, z + d, core))

    def stage_d(t):
        landed(yrx2.at[t, 0], r_y2.at[t, 0])
        landed(yrx2.at[t, 1], r_y2.at[t, 1])
        total = part[t, y] + yrx2[t, 0].astype(F32) + yrx2[t, 1].astype(F32)
        ztx[t] = total.reshape(nz, seg, cols)

        def send(d, carry):
            z_copy(t, d).start()
            return carry

        lax.fori_loop(1, nz, send, 0)

    def g_copy(t, d):
        mine = xt.at[t, y, pl.ds(pl.multiple_of(core * half + z * seg, seg), seg), :]
        return copy(mine, mine, s_gz.at[t, d], r_gz.at[t, d], at(y, z + d, core))

    def stage_e(t):
        def add(d, total):
            landed(zrx.at[t, d], r_z.at[t, d])
            return total + zrx[t, d]

        total = lax.fori_loop(1, nz, add, ztx[t, z])
        xt[t, y, pl.ds(pl.multiple_of(core * half + z * seg, seg), seg), :] = total.astype(BF16)

        def send(d, carry):
            g_copy(t, d).start()
            return carry

        lax.fori_loop(1, nz, send, 0)

    def half_of(t, y_, start, size):
        first = pl.multiple_of(core * half + start, mid)
        return xt.at[t, lax.rem(y_ + NY, NY), pl.ds(first, size), :]

    def stage_f(t):
        def wait(d, carry):
            g_copy(t, d).wait_recv()
            return carry

        lax.fori_loop(1, nz, wait, 0)
        mine = half_of(t, y, 0, half)
        go(mine, mine, s_gy.at[t, 0], r_gy.at[t, 0], up)
        go(mine, mine, s_gy.at[t, 1], r_gy.at[t, 1], down)
        go(mine, mine, s_gs.at[t, 0], r_gs.at[t, 0], sib)

    def stage_g(t):
        landed(half_of(t, y - 1, 0, half), r_gy.at[t, 0])
        piece = half_of(t, y - 1, 0, mid)
        go(piece, piece, s_gy.at[t, 2], r_gy.at[t, 2], up)
        landed(half_of(t, y + 1, 0, half), r_gy.at[t, 1])
        piece = half_of(t, y + 1, mid, mid)
        go(piece, piece, s_gy.at[t, 3], r_gy.at[t, 3], down)
        for k, d in ((1, -1), (2, 1)):
            piece = half_of(t, y + d, 0, half)
            go(piece, piece, s_gs.at[t, k], r_gs.at[t, k], sib)

    def stage_h(t):
        landed(half_of(t, y + 2, 0, mid), r_gy.at[t, 2])
        landed(half_of(t, y + 2, mid, mid), r_gy.at[t, 3])
        piece = half_of(t, y + 2, 0, half)
        go(piece, piece, s_gs.at[t, 3], r_gs.at[t, 3], sib)

    def stage_i(t):
        for k in range(4):
            landed(half_of(t, y, 0, half), r_gs.at[t, k])

        def block(b, carry):
            got = jnp.dot(
                xt[t, b], f_ref[pl.ds(pl.multiple_of(b * cols, cols), cols), :],
                preferred_element_type=F32,
            )
            acc[min(t, 1)] = jnp.where(b == 0, got, acc[min(t, 1)] + got)
            return carry

        lax.fori_loop(0, NY, block, 0)
        if t:
            ptx[t - 1] = acc[1].astype(BF16)
        if t == 1:
            go(ptx.at[0], prx.at[1], s_p.at[1], r_p.at[1], left)
        if t == 2:
            go(ptx.at[1], prx.at[0], s_p.at[0], r_p.at[0], right)
        if t == 3:
            go(ptx.at[2, :half], relay.at[0], s_p.at[2], r_p.at[2], right)
            go(ptx.at[2, half:], relay.at[1], s_p.at[3], r_p.at[3], left)

    stages = (
        stage_a, stage_b, stage_c, stage_d, stage_e, stage_f, stage_g, stage_h, stage_i,
    )
    for step in range(len(stages) + nx - 1):
        for k in reversed(range(len(stages))):
            if 0 <= step - k < nx:
                stages[k](step - k)

    landed(relay.at[0], r_p.at[2])
    go(relay.at[0], prx.at[2, :half], s_p.at[4], r_p.at[4], right)
    landed(relay.at[1], r_p.at[3])
    go(relay.at[1], prx.at[2, half:], s_p.at[5], r_p.at[5], left)
    landed(prx.at[0], r_p.at[0])
    landed(prx.at[1], r_p.at[1])
    landed(prx.at[2, :half], r_p.at[4])
    landed(prx.at[2, half:], r_p.at[5])
    total = acc[0] + prx[0].astype(F32) + prx[1].astype(F32) + prx[2].astype(F32)
    out_ref[...] = total.astype(BF16)
    for c in sent:
        c.wait_send()
    for t in range(nx):
        def drain(d, carry, t=t):
            z_copy(t, d).wait_send()
            g_copy(t, d).wait_send()
            return carry

        lax.fori_loop(1, nz, drain, 0)


def middle(factors, weights):
    rows, width = weights.shape
    nx = lax.axis_size("aux")
    nz = lax.axis_size("pair") // (2 * NY)
    half, cols = rows // 2, factors.shape[0] // NY
    seg, mid = half // nz, half // 2
    dma = pltpu.SemaphoreType.DMA
    vmem = pl.BlockSpec(memory_space=pltpu.VMEM)
    pairs = [(4,), (nx,), (nx, 2), (nx, 2), (nx, nz), (nx, nz), (nx, 4), (nx, 4), (6,)]
    return pl.pallas_call(
        functools.partial(middle_kernel, nz, nx),
        out_shape=jax.ShapeDtypeStruct((rows, width), BF16),
        in_specs=[vmem, vmem],
        out_specs=vmem,
        scratch_shapes=[
            pltpu.VMEM((3, rows, width), BF16),
            pltpu.VMEM((nx, NY, half, cols), BF16),
            pltpu.VMEM((nx, NY, half, cols), BF16),
            pltpu.VMEM((nx, NY, half, cols), F32),
            pltpu.VMEM((nx, half, cols), BF16),
            pltpu.VMEM((nx, 2, mid, cols), BF16),
            pltpu.VMEM((nx, 2, half, cols), BF16),
            pltpu.VMEM((nx, 2, half, cols), BF16),
            pltpu.VMEM((nx, nz, seg, cols), F32),
            pltpu.VMEM((nx, nz, seg, cols), F32),
            pltpu.VMEM((nx, NY, rows, cols), BF16),
            pltpu.VMEM((3, rows, width), BF16),
            pltpu.VMEM((3, rows, width), BF16),
            pltpu.VMEM((2, half, width), BF16),
            pltpu.VMEM((2, rows, width), F32),
        ]
        + [dma(shape) for shape in pairs for _ in range(2)],
        compiler_params=pltpu.CompilerParams(
            collective_id=0, has_side_effects=True, vmem_limit_bytes=56 << 20
        ),
        cost_estimate=pl.CostEstimate(
            flops=4 * nx * rows * width * factors.shape[0], bytes_accessed=8 << 20, transcendentals=0
        ),
    )(factors, weights)


def on_device(factors, amplitudes, block_list, owner_map):
    pair_count = lax.axis_size("pair")
    aux_count = lax.axis_size("aux")
    me = lax.axis_index("pair")
    share = lax.axis_index("aux")
    block_count, block_width, _ = amplitudes.shape
    virt = factors.shape[2]
    part = block_width // aux_count
    slot_total = pair_count * CAP
    ids = lax.iota(jnp.int32, block_count)
    hits = block_list[:, 0][:, None] == lax.iota(jnp.int32, owner_map.shape[0])[None, :]
    owners = jnp.sum(jnp.where(hits, owner_map[None, :], 0), axis=1)
    codes = owners * (virt * virt) + block_list[:, 1] * virt + block_list[:, 2]
    same = (owners[:, None] == owners[None, :]) & (ids[None, :] < ids[:, None])
    slots = owners * CAP + jnp.sum(same.astype(jnp.int32), axis=1)
    placing = (slots[:, None] == lax.iota(jnp.int32, slot_total)[None, :]).astype(BF16)
    all_codes = lax.all_gather(codes, "pair", axis=0, tiled=False)
    mine = lax.dynamic_slice_in_dim(amplitudes, share * part, part, axis=1)
    sent = jnp.einsum("js,jm->sm", placing, mine.reshape(block_count, -1), preferred_element_type=F32)
    sent = sent.astype(BF16).reshape(pair_count, CAP, part, block_width)
    got = lax.all_to_all(sent, "pair", split_axis=0, concat_axis=0, tiled=True)
    ours = all_codes // (virt * virt) == me
    combos = all_codes % (virt * virt)
    first = jnp.min(jnp.where(ours, ids[None, :], block_count), axis=1)
    last = jnp.max(jnp.where(ours, ids[None, :], -1), axis=1)
    at_first = ours & (ids[None, :] == first[:, None])
    at_second = ours & (ids[None, :] == last[:, None]) & (last > first)[:, None]
    combo0 = jnp.sum(jnp.where(at_first, combos + 1, 0), axis=1) - 1
    combo1 = jnp.sum(jnp.where(at_second, combos + 1, 0), axis=1) - 1
    slot_combo = jnp.stack([combo0, combo1], axis=1).reshape(slot_total)
    picks = (slot_combo[:, None] == lax.iota(jnp.int32, virt * virt)[None, :]).astype(BF16)
    weights = jnp.einsum(
        "sn,sm->nm", picks, got.reshape(slot_total, -1), preferred_element_type=F32
    ).astype(BF16)
    weights = weights.reshape(virt, virt, part, block_width).transpose(0, 2, 1, 3)
    out = middle(
        factors.reshape(-1, virt * block_width), weights.reshape(virt * part, virt * block_width)
    )
    out = out.astype(BF16).reshape(virt, part, virt, block_width).transpose(0, 2, 1, 3)
    back = jnp.einsum(
        "sn,nm->sm", picks, out.reshape(virt * virt, -1), preferred_element_type=F32
    )
    back = back.astype(BF16).reshape(pair_count, CAP, part, block_width)
    back = lax.all_to_all(back, "pair", split_axis=0, concat_axis=0, tiled=True)
    result = jnp.einsum(
        "js,sm->jm", placing, back.reshape(slot_total, -1), preferred_element_type=F32
    )
    result = result.astype(BF16).reshape(block_count, part, block_width)
    return lax.all_gather(result, "aux", axis=1, tiled=True)


def solution(mesh):
    placed = (P("pair", "aux", None, None), P("pair", None, None), P("pair", None), P())
    return jax.shard_map(
        on_device, mesh=mesh, in_specs=placed, out_specs=P("pair", None, None), check_vma=False
    )
```

```python
import functools

import jax
import jax.numpy as jnp
from jax import lax
from jax.experimental import pallas as pl
from jax.experimental.pallas import tpu as pltpu
from jax.sharding import PartitionSpec as P

CAP = 2
NY = 4
F32 = jnp.float32
BF16 = jnp.bfloat16
MESH = pl.DeviceIdType.MESH
NT = (((1,), (1,)), ((), ()))


def middle_kernel(
    nz, nx, f_ref, w_ref, out_ref, wall, sibtx, sibrx, part, ytx1, yrx1, ytx2, yrx2, ztx, zrx, xt,
    ptx, prx, relay, acc, s_w, r_w, s_sib, r_sib, s_y1, r_y1, s_y2, r_y2, s_z, r_z, s_gz, r_gz,
    s_gy, r_gy, s_gs, r_gs, s_p, r_p,
):
    pair, aux = lax.axis_index("pair"), lax.axis_index("aux")
    core, z, y = lax.rem(pair, 2), lax.rem(pair // 2, nz), pair // (2 * nz)
    half = sibtx.shape[2]
    seg = half // nz
    mid = half // 2
    cols = part.shape[3]
    rows = 2 * half

    def at(y_, z_, c_):
        return {"pair": (lax.rem(y_ + NY, NY) * nz + lax.rem(z_ + nz, nz)) * 2 + c_}

    sib = at(y, z, 1 - core)
    up, down = at(y + 1, z, core), at(y - 1, z, core)
    right, left = {"aux": lax.rem(aux + 1, nx)}, {"aux": lax.rem(aux + nx - 1, nx)}

    def copy(src, dst, send, recv, to):
        return pltpu.make_async_remote_copy(
            src_ref=src, dst_ref=dst, send_sem=send, recv_sem=recv, device_id=to, device_id_type=MESH
        )

    barrier = pltpu.get_barrier_semaphore()
    for peer in (sib, up, down, right, left):
        pl.semaphore_signal(barrier, inc=1, device_id=peer, device_id_type=MESH)

    def greet(d, carry):
        pl.semaphore_signal(barrier, inc=1, device_id=at(y, z + d, core), device_id_type=MESH)
        return carry

    lax.fori_loop(1, nz, greet, 0)
    pl.semaphore_wait(barrier, 5 + nz - 1)

    sent = []

    def go(*args):
        c = copy(*args)
        c.start()
        sent.append(c)
        return c

    go(w_ref, wall.at[0], s_w.at[0], r_w.at[0], right)
    go(w_ref, wall.at[1], s_w.at[1], r_w.at[1], left)

    def landed(dst, recv):
        copy(dst, dst, recv, recv, sib).wait_recv()

    own = pl.multiple_of(core * half, half)
    other = pl.multiple_of((1 - core) * half, half)

    def weights_product(t):
        if t == 1:
            landed(wall.at[0], r_w.at[0])
            go(wall.at[0, :half], wall.at[2, :half], s_w.at[2], r_w.at[2], right)
            landed(wall.at[1], r_w.at[1])
            go(wall.at[1, half:], wall.at[2, half:], s_w.at[3], r_w.at[3], left)
        if t == 3:
            landed(wall.at[2, :half], r_w.at[2])
            landed(wall.at[2, half:], r_w.at[3])
        w = w_ref if t == 0 else wall.at[t - 1]
        w_both = jnp.concatenate([w[pl.ds(other, half), :], w[pl.ds(own, half), :]], axis=0)

        def block(b, carry):
            got = lax.dot_general(
                w_both, f_ref[pl.ds(pl.multiple_of(b * cols, cols), cols), :], NT,
                preferred_element_type=F32,
            )
            sibtx[t, b] = got[:half].astype(BF16)
            part[t, b] = got[half:]
            return carry

        lax.fori_loop(0, NY, block, 0)
        go(sibtx.at[t], sibrx.at[t], s_sib.at[t], r_sib.at[t], sib)

    def core_sum(t):
        landed(sibrx.at[t], r_sib.at[t])

        def block(b, carry):
            part[t, b] = part[t, b] + sibrx[t, b].astype(F32)
            return carry

        lax.fori_loop(0, NY, block, 0)
        ytx1[t] = part[t, lax.rem(y + 2, NY)].astype(BF16)
        go(ytx1.at[t, :mid], yrx1.at[t, 0], s_y1.at[t, 0], r_y1.at[t, 0], up)
        go(ytx1.at[t, mid:], yrx1.at[t, 1], s_y1.at[t, 1], r_y1.at[t, 1], down)

    def y_relay_sum(t):
        above, below = lax.rem(y + 1, NY), lax.rem(y + NY - 1, NY)
        landed(yrx1.at[t, 0], r_y1.at[t, 0])
        ytx2[t, 0, :mid] = (part[t, above, :mid] + yrx1[t, 0].astype(F32)).astype(BF16)
        ytx2[t, 0, mid:] = part[t, above, mid:].astype(BF16)
        go(ytx2.at[t, 0], yrx2.at[t, 0], s_y2.at[t, 0], r_y2.at[t, 0], up)
        landed(yrx1.at[t, 1], r_y1.at[t, 1])
        ytx2[t, 1, :mid] = part[t, below, :mid].astype(BF16)
        ytx2[t, 1, mid:] = (part[t, below, mid:] + yrx1[t, 1].astype(F32)).astype(BF16)
        go(ytx2.at[t, 1], yrx2.at[t, 1], s_y2.at[t, 1], r_y2.at[t, 1], down)

    def z_copy(t, d):
        to = lax.rem(z + d, nz)
        return copy(ztx.at[t, to], zrx.at[t, d], s_z.at[t, d], r_z.at[t, d], at(y, z + d, core))

    def y_sum(t):
        landed(yrx2.at[t, 0], r_y2.at[t, 0])
        landed(yrx2.at[t, 1], r_y2.at[t, 1])
        total = part[t, y] + yrx2[t, 0].astype(F32) + yrx2[t, 1].astype(F32)
        ztx[t] = total.reshape(nz, seg, cols)

        def send(d, carry):
            z_copy(t, d).start()
            return carry

        lax.fori_loop(1, nz, send, 0)

    def g_copy(t, d):
        mine = xt.at[t, y, pl.ds(pl.multiple_of(core * half + z * seg, seg), seg), :]
        return copy(mine, mine, s_gz.at[t, d], r_gz.at[t, d], at(y, z + d, core))

    def z_sum(t):
        def add(d, total):
            landed(zrx.at[t, d], r_z.at[t, d])
            return total + zrx[t, d]

        total = lax.fori_loop(1, nz, add, ztx[t, z])
        xt[t, y, pl.ds(pl.multiple_of(core * half + z * seg, seg), seg), :] = total.astype(BF16)

        def send(d, carry):
            g_copy(t, d).start()
            return carry

        lax.fori_loop(1, nz, send, 0)

    def half_of(t, y_, start, size):
        first = pl.multiple_of(core * half + start, mid)
        return xt.at[t, lax.rem(y_ + NY, NY), pl.ds(first, size), :]

    def z_gather(t):
        def wait(d, carry):
            g_copy(t, d).wait_recv()
            return carry

        lax.fori_loop(1, nz, wait, 0)
        mine = half_of(t, y, 0, half)
        go(mine, mine, s_gy.at[t, 0], r_gy.at[t, 0], up)
        go(mine, mine, s_gy.at[t, 1], r_gy.at[t, 1], down)
        go(mine, mine, s_gs.at[t, 0], r_gs.at[t, 0], sib)

    def y_gather(t):
        landed(half_of(t, y - 1, 0, half), r_gy.at[t, 0])
        piece = half_of(t, y - 1, 0, mid)
        go(piece, piece, s_gy.at[t, 2], r_gy.at[t, 2], up)
        landed(half_of(t, y + 1, 0, half), r_gy.at[t, 1])
        piece = half_of(t, y + 1, mid, mid)
        go(piece, piece, s_gy.at[t, 3], r_gy.at[t, 3], down)
        for k, d in ((1, -1), (2, 1)):
            piece = half_of(t, y + d, 0, half)
            go(piece, piece, s_gs.at[t, k], r_gs.at[t, k], sib)

    def y_relay_gather(t):
        landed(half_of(t, y + 2, 0, mid), r_gy.at[t, 2])
        landed(half_of(t, y + 2, mid, mid), r_gy.at[t, 3])
        piece = half_of(t, y + 2, 0, half)
        go(piece, piece, s_gs.at[t, 3], r_gs.at[t, 3], sib)

    def block_product(t):
        for k in range(4):
            landed(half_of(t, y, 0, half), r_gs.at[t, k])

        def block(b, carry):
            got = jnp.dot(
                xt[t, b], f_ref[pl.ds(pl.multiple_of(b * cols, cols), cols), :],
                preferred_element_type=F32,
            )
            acc[min(t, 1)] = jnp.where(b == 0, got, acc[min(t, 1)] + got)
            return carry

        lax.fori_loop(0, NY, block, 0)
        if t:
            ptx[t - 1] = acc[1].astype(BF16)
        if t == 1:
            go(ptx.at[0], prx.at[1], s_p.at[1], r_p.at[1], left)
        if t == 2:
            go(ptx.at[1], prx.at[0], s_p.at[0], r_p.at[0], right)
        if t == 3:
            go(ptx.at[2, :half], relay.at[0], s_p.at[2], r_p.at[2], right)
            go(ptx.at[2, half:], relay.at[1], s_p.at[3], r_p.at[3], left)

    stages = (
        weights_product, core_sum, y_relay_sum, y_sum, z_sum, z_gather, y_gather, y_relay_gather, block_product,
    )
    for step in range(len(stages) + nx - 1):
        for k in reversed(range(len(stages))):
            if 0 <= step - k < nx:
                with jax.named_scope(f"{stages[k].__name__}_chunk{step - k}"):
                    stages[k](step - k)

    landed(relay.at[0], r_p.at[2])
    go(relay.at[0], prx.at[2, :half], s_p.at[4], r_p.at[4], right)
    landed(relay.at[1], r_p.at[3])
    go(relay.at[1], prx.at[2, half:], s_p.at[5], r_p.at[5], left)
    landed(prx.at[0], r_p.at[0])
    landed(prx.at[1], r_p.at[1])
    landed(prx.at[2, :half], r_p.at[4])
    landed(prx.at[2, half:], r_p.at[5])
    total = acc[0] + prx[0].astype(F32) + prx[1].astype(F32) + prx[2].astype(F32)
    out_ref[...] = total.astype(BF16)
    for c in sent:
        c.wait_send()
    for t in range(nx):
        def drain(d, carry, t=t):
            z_copy(t, d).wait_send()
            g_copy(t, d).wait_send()
            return carry

        lax.fori_loop(1, nz, drain, 0)


def middle(factors, weights):
    rows, width = weights.shape
    nx = lax.axis_size("aux")
    nz = lax.axis_size("pair") // (2 * NY)
    half, cols = rows // 2, factors.shape[0] // NY
    seg, mid = half // nz, half // 2
    dma = pltpu.SemaphoreType.DMA
    vmem = pl.BlockSpec(memory_space=pltpu.VMEM)
    pairs = [(4,), (nx,), (nx, 2), (nx, 2), (nx, nz), (nx, nz), (nx, 4), (nx, 4), (6,)]
    return pl.pallas_call(
        functools.partial(middle_kernel, nz, nx),
        out_shape=jax.ShapeDtypeStruct((rows, width), BF16),
        in_specs=[vmem, vmem],
        out_specs=vmem,
        scratch_shapes=[
            pltpu.VMEM((3, rows, width), BF16),
            pltpu.VMEM((nx, NY, half, cols), BF16),
            pltpu.VMEM((nx, NY, half, cols), BF16),
            pltpu.VMEM((nx, NY, half, cols), F32),
            pltpu.VMEM((nx, half, cols), BF16),
            pltpu.VMEM((nx, 2, mid, cols), BF16),
            pltpu.VMEM((nx, 2, half, cols), BF16),
            pltpu.VMEM((nx, 2, half, cols), BF16),
            pltpu.VMEM((nx, nz, seg, cols), F32),
            pltpu.VMEM((nx, nz, seg, cols), F32),
            pltpu.VMEM((nx, NY, rows, cols), BF16),
            pltpu.VMEM((3, rows, width), BF16),
            pltpu.VMEM((3, rows, width), BF16),
            pltpu.VMEM((2, half, width), BF16),
            pltpu.VMEM((2, rows, width), F32),
        ]
        + [dma(shape) for shape in pairs for _ in range(2)],
        compiler_params=pltpu.CompilerParams(
            collective_id=0, has_side_effects=True, vmem_limit_bytes=56 << 20
        ),
        cost_estimate=pl.CostEstimate(
            flops=4 * nx * rows * width * factors.shape[0], bytes_accessed=8 << 20, transcendentals=0
        ),
    )(factors, weights)

def exchange_kernel(n, send_ref, meta_ref, f_ref, got_ref, gmeta_ref, flat_ref, s_d, r_d, s_m, r_m):
    me = lax.axis_index("pair")
    barrier = pltpu.get_barrier_semaphore()

    def greet(d, carry):
        pl.semaphore_signal(
            barrier, inc=1, device_id={"pair": lax.rem(me + d, n)}, device_id_type=MESH
        )
        return carry

    lax.fori_loop(1, n, greet, 0)
    pl.semaphore_wait(barrier, n - 1)

    def copies(d):
        to = lax.rem(me + d, n)
        return (
            pltpu.make_async_remote_copy(
                src_ref=meta_ref.at[to], dst_ref=gmeta_ref.at[me], send_sem=s_m.at[d],
                recv_sem=r_m.at[d], device_id={"pair": to}, device_id_type=MESH,
            ),
            pltpu.make_async_remote_copy(
                src_ref=send_ref.at[to], dst_ref=got_ref.at[me], send_sem=s_d.at[d],
                recv_sem=r_d.at[d], device_id={"pair": to}, device_id_type=MESH,
            ),
        )

    def start(d, carry):
        for c in copies(d):
            c.start()
        return carry

    lax.fori_loop(1, n, start, 0)
    got_ref[me] = send_ref[me]
    gmeta_ref[me] = meta_ref[me]
    step = 64 if f_ref.shape[0] % 64 == 0 else f_ref.shape[0]

    def flatten(i, carry):
        rows = pl.ds(pl.multiple_of(i * step, step), step)
        flat_ref[rows, :] = f_ref[rows].astype(F32).reshape(step, -1).astype(BF16)
        return carry

    lax.fori_loop(0, f_ref.shape[0] // step, flatten, 0)

    def finish(d, carry):
        for c in copies(d):
            c.wait()
        return carry

    lax.fori_loop(1, n, finish, 0)


def exchange(send, meta, factors):
    n = send.shape[0]
    dma = pltpu.SemaphoreType.DMA
    vmem = pl.BlockSpec(memory_space=pltpu.VMEM)
    return pl.pallas_call(
        functools.partial(exchange_kernel, n),
        out_shape=(
            jax.ShapeDtypeStruct(send.shape, send.dtype),
            jax.ShapeDtypeStruct(meta.shape, meta.dtype),
            jax.ShapeDtypeStruct((factors.shape[0], factors.shape[1] * factors.shape[2]), BF16),
        ),
        in_specs=[vmem] * 3,
        out_specs=(vmem,) * 3,
        scratch_shapes=[dma((n,))] * 4,
        compiler_params=pltpu.CompilerParams(
            collective_id=1, has_side_effects=True, vmem_limit_bytes=40 << 20
        ),
    )(send, meta, factors)


def back_kernel(n, send_ref, got_ref, s_d, r_d):
    me = lax.axis_index("pair")
    barrier = pltpu.get_barrier_semaphore()

    def greet(d, carry):
        pl.semaphore_signal(
            barrier, inc=1, device_id={"pair": lax.rem(me + d, n)}, device_id_type=MESH
        )
        return carry

    lax.fori_loop(1, n, greet, 0)
    pl.semaphore_wait(barrier, n - 1)

    def message(d):
        to = lax.rem(me + d, n)
        return pltpu.make_async_remote_copy(
            src_ref=send_ref.at[to], dst_ref=got_ref.at[me], send_sem=s_d.at[d],
            recv_sem=r_d.at[d], device_id={"pair": to}, device_id_type=MESH,
        )

    def start(d, carry):
        message(d).start()
        return carry

    lax.fori_loop(1, n, start, 0)
    got_ref[me] = send_ref[me]

    def finish(d, carry):
        message(d).wait()
        return carry

    lax.fori_loop(1, n, finish, 0)


def send_back(send):
    n = send.shape[0]
    dma = pltpu.SemaphoreType.DMA
    vmem = pl.BlockSpec(memory_space=pltpu.VMEM)
    return pl.pallas_call(
        functools.partial(back_kernel, n),
        out_shape=jax.ShapeDtypeStruct(send.shape, send.dtype),
        in_specs=[vmem],
        out_specs=vmem,
        scratch_shapes=[dma((n,))] * 2,
        compiler_params=pltpu.CompilerParams(
            collective_id=2, has_side_effects=True, vmem_limit_bytes=24 << 20
        ),
    )(send)


def join_kernel(nx, part_ref, out_ref, s_d, r_d):
    aux = lax.axis_index("aux")
    right, left = {"aux": lax.rem(aux + 1, nx)}, {"aux": lax.rem(aux + nx - 1, nx)}
    barrier = pltpu.get_barrier_semaphore()
    for peer in (right, left):
        pl.semaphore_signal(barrier, inc=1, device_id=peer, device_id_type=MESH)
    pl.semaphore_wait(barrier, 2)
    count, part, _ = part_ref.shape
    half = count // 2

    def place(who, first, size):
        rows = pl.ds(pl.multiple_of(lax.rem(who + nx, nx) * part, part), part)
        return out_ref.at[pl.ds(first, size), rows, :]

    def copy(src, dst, k, to):
        return pltpu.make_async_remote_copy(
            src_ref=src, dst_ref=dst, send_sem=s_d.at[k], recv_sem=r_d.at[k], device_id=to,
            device_id_type=MESH,
        )

    own = [
        copy(part_ref.at[:half], place(aux, 0, half), 0, right),
        copy(part_ref.at[half:], place(aux, half, half), 1, left),
        copy(part_ref.at[half:], place(aux, half, half), 2, right),
        copy(part_ref.at[:half], place(aux, 0, half), 3, left),
    ]
    for c in own:
        c.start()
    out_ref[:, pl.ds(pl.multiple_of(aux * part, part), part), :] = part_ref[...]
    low, high = place(aux - 1, 0, half), place(aux + 1, half, half)
    on = [copy(low, low, 4, right), copy(high, high, 5, left)]
    own[0].wait_recv()
    on[0].start()
    own[1].wait_recv()
    on[1].start()
    for c in own[2:] + on:
        c.wait_recv()
    for c in own + on:
        c.wait_send()


def join(part):
    nx = lax.axis_size("aux")
    count, rows, width = part.shape
    dma = pltpu.SemaphoreType.DMA
    vmem = pl.BlockSpec(memory_space=pltpu.VMEM)
    return pl.pallas_call(
        functools.partial(join_kernel, nx),
        out_shape=jax.ShapeDtypeStruct((count, nx * rows, width), part.dtype),
        in_specs=[vmem],
        out_specs=vmem,
        scratch_shapes=[dma((6,))] * 2,
        compiler_params=pltpu.CompilerParams(
            collective_id=3, has_side_effects=True, vmem_limit_bytes=24 << 20
        ),
    )(part)


def on_device(factors, amplitudes, block_list, owner_map):
    pair_count = lax.axis_size("pair")
    aux_count = lax.axis_size("aux")
    share = lax.axis_index("aux")
    block_count, block_width, _ = amplitudes.shape
    virt = factors.shape[2]
    combos = virt * virt
    part = block_width // aux_count
    slot_total = pair_count * CAP
    ids = lax.iota(jnp.int32, block_count)
    hits = block_list[:, 0][:, None] == lax.iota(jnp.int32, owner_map.shape[0])[None, :]
    owners = jnp.sum(jnp.where(hits, owner_map[None, :], 0), axis=1)
    combo = block_list[:, 1] * virt + block_list[:, 2]
    same = (owners[:, None] == owners[None, :]) & (ids[None, :] < ids[:, None])
    slots = owners * CAP + jnp.sum(same.astype(jnp.int32), axis=1)
    placing = (slots[:, None] == lax.iota(jnp.int32, slot_total)[None, :]).astype(BF16)
    at_combo = (combo[:, None] == lax.iota(jnp.int32, combos)[None, :]).astype(BF16)
    picks_out = jnp.einsum("js,jn->sn", placing, at_combo, preferred_element_type=F32)
    mine = lax.dynamic_slice_in_dim(amplitudes, share * part, part, axis=1)
    sent = jnp.einsum("js,jm->sm", placing, mine.reshape(block_count, -1), preferred_element_type=F32)
    sent = sent.astype(BF16).reshape(pair_count, CAP, part, block_width)
    got, picks, flat = exchange(
        sent, picks_out.reshape(pair_count, 1, CAP * combos), factors.reshape(-1, virt, block_width)
    )
    picks = picks.reshape(slot_total, combos).astype(BF16)
    weights = jnp.einsum(
        "sn,sm->nm", picks, got.reshape(slot_total, -1), preferred_element_type=F32
    ).astype(BF16)
    weights = weights.reshape(virt, virt, part, block_width).transpose(0, 2, 1, 3)
    out = middle(flat, weights.reshape(virt * part, virt * block_width))
    out = out.reshape(virt, part, virt, block_width).transpose(0, 2, 1, 3)
    back = jnp.einsum(
        "sn,nm->sm", picks, out.reshape(combos, -1), preferred_element_type=F32
    )
    back = send_back(back.astype(BF16).reshape(pair_count, CAP, part, block_width))
    result = jnp.einsum(
        "js,sm->jm", placing, back.reshape(slot_total, -1), preferred_element_type=F32
    )
    return join(result.astype(BF16).reshape(block_count, part, block_width))


def solution(mesh):
    placed = (P("pair", "aux", None, None), P("pair", None, None), P("pair", None), P())
    return jax.shard_map(
        on_device, mesh=mesh, in_specs=placed, out_specs=P("pair", None, None), check_vma=False
    )
```

```python
import functools

import jax
import jax.numpy as jnp
from jax import lax
from jax.experimental import pallas as pl
from jax.experimental.pallas import tpu as pltpu
from jax.sharding import PartitionSpec as P

CAP = 2
NY = 4
F32 = jnp.float32
BF16 = jnp.bfloat16
MESH = pl.DeviceIdType.MESH
NT = (((1,), (1,)), ((), ()))
TN = (((0,), (0,)), ((), ()))


def cycle_kernel(
    nz, nx, factor_ref, send_ref, meta_ref, place_ref, out_ref, f_ref, got_ref, picks_ref, bsend,
    bgot, w_ref, wall, sibtx, sibrx, part, ytx1, yrx1, ytx2, yrx2, ztx, zrx, xt, ptx, prx, relay,
    acc, s_m, r_m, s_a, r_a, s_b, r_b, s_j, r_j, s_w, r_w, s_sib, r_sib, s_y1, r_y1, s_y2, r_y2,
    s_z, r_z, s_gz, r_gz, s_gy, r_gy, s_gs, r_gs, s_p, r_p,
):
    pair, aux = lax.axis_index("pair"), lax.axis_index("aux")
    core, z, y = lax.rem(pair, 2), lax.rem(pair // 2, nz), pair // (2 * nz)
    half = sibtx.shape[2]
    seg = half // nz
    mid = half // 2
    cols = part.shape[3]
    rows = 2 * half

    def at(y_, z_, c_):
        return {"pair": (lax.rem(y_ + NY, NY) * nz + lax.rem(z_ + nz, nz)) * 2 + c_}

    sib = at(y, z, 1 - core)
    up, down = at(y + 1, z, core), at(y - 1, z, core)
    right, left = {"aux": lax.rem(aux + 1, nx)}, {"aux": lax.rem(aux + nx - 1, nx)}

    def copy(src, dst, send, recv, to):
        return pltpu.make_async_remote_copy(
            src_ref=src, dst_ref=dst, send_sem=send, recv_sem=recv, device_id=to, device_id_type=MESH
        )

    n = 2 * NY * nz
    barrier = pltpu.get_barrier_semaphore()
    for peer in (right, left):
        pl.semaphore_signal(barrier, inc=1, device_id=peer, device_id_type=MESH)

    def peer_at(d):
        return lax.rem(pair + d, n)

    def greet(d, carry):
        pl.semaphore_signal(
            barrier, inc=1, device_id={"pair": peer_at(d)}, device_id_type=MESH
        )
        return carry

    lax.fori_loop(1, n, greet, 0)
    pl.semaphore_wait(barrier, n + 1)

    sent = []

    def go(*args):
        c = copy(*args)
        c.start()
        sent.append(c)
        return c

    def landed(dst, recv):
        copy(dst, dst, recv, recv, sib).wait_recv()

    thin = send_ref.shape[2] // 2
    width = send_ref.shape[3]
    virt = w_ref.shape[1] // width

    def meta_copy(d):
        to = peer_at(d)
        return copy(
            meta_ref.at[to], picks_ref.at[pair], s_m.at[d], r_m.at[d], {"pair": to}
        )

    def out_copy(h, d):
        to = peer_at(d)
        return copy(
            send_ref.at[to, :, h * thin : (h + 1) * thin, :], got_ref.at[h, pair], s_a.at[h, d],
            r_a.at[h, d], {"pair": to},
        )

    def back_copy(h, d):
        to = peer_at(d)
        return copy(bsend.at[h, to], bgot.at[h, pair], s_b.at[h, d], r_b.at[h, d], {"pair": to})

    def each_peer(act):
        def one(d, carry):
            act(d)
            return carry

        lax.fori_loop(1, n, one, 0)

    def first(d):
        meta_copy(d).start()
        out_copy(0, d).start()

    each_peer(first)
    each_peer(lambda d: out_copy(1, d).start())
    picks_ref[pair] = meta_ref[pair]
    for h in range(2):
        got_ref[h, pair] = send_ref[pair, :, h * thin : (h + 1) * thin, :]
    step = 64 if f_ref.shape[0] % 64 == 0 else f_ref.shape[0]

    def flatten(i, carry):
        at_rows = pl.ds(pl.multiple_of(i * step, step), step)
        f_ref[at_rows, :] = factor_ref[at_rows].astype(F32).reshape(step, -1).astype(BF16)
        return carry

    lax.fori_loop(0, f_ref.shape[0] // step, flatten, 0)

    def combine(h):
        total = 0.0
        for r in range(CAP):
            rows_r = got_ref[h, :, r].astype(F32).reshape(n, thin * width).astype(BF16)
            total = total + lax.dot_general(
                picks_ref[:, r, :].astype(BF16), rows_r, TN, preferred_element_type=F32
            )
        total = total[: virt * virt].reshape(virt * virt, thin, width).astype(BF16)
        for a in range(virt):
            for c in range(virt):
                low = h * half + a * thin
                w_ref[low : low + thin, c * width : (c + 1) * width] = total[a * virt + c]
        piece = slice(h * half, (h + 1) * half)
        go(w_ref.at[piece], wall.at[0, piece], s_w.at[2 * h], r_w.at[2 * h], right)
        go(w_ref.at[piece], wall.at[1, piece], s_w.at[2 * h + 1], r_w.at[2 * h + 1], left)

    each_peer(lambda d: meta_copy(d).wait_recv())
    each_peer(lambda d: out_copy(0, d).wait_recv())
    combine(0)
    landed(wall.at[0, :half], r_w.at[0])
    go(wall.at[0, :half], wall.at[2, :half], s_w.at[4], r_w.at[4], right)
    each_peer(lambda d: out_copy(1, d).wait_recv())
    combine(1)

    own = pl.multiple_of(core * half, half)
    other = pl.multiple_of((1 - core) * half, half)

    def weights_product(t):
        if t == 0:
            landed(wall.at[1, half:], r_w.at[3])
            go(wall.at[1, half:], wall.at[2, half:], s_w.at[5], r_w.at[5], left)
            landed(wall.at[0, half:], r_w.at[2])
        if t == 1:
            landed(wall.at[1, :half], r_w.at[1])
        if t == 2:
            landed(wall.at[2, :half], r_w.at[4])
            landed(wall.at[2, half:], r_w.at[5])
        w = w_ref if t == 3 else wall.at[t]
        w_both = jnp.concatenate([w[pl.ds(other, half), :], w[pl.ds(own, half), :]], axis=0)

        def block(b, carry):
            got = lax.dot_general(
                w_both, f_ref[pl.ds(pl.multiple_of(b * cols, cols), cols), :], NT,
                preferred_element_type=F32,
            )
            sibtx[t, b] = got[:half]
            part[t, b] = got[half:]
            return carry

        lax.fori_loop(0, NY, block, 0)
        go(sibtx.at[t], sibrx.at[t], s_sib.at[t], r_sib.at[t], sib)

    def core_sum(t):
        landed(sibrx.at[t], r_sib.at[t])

        def block(b, carry):
            part[t, b] = part[t, b] + sibrx[t, b]
            return carry

        lax.fori_loop(0, NY, block, 0)
        ytx1[t] = part[t, lax.rem(y + 2, NY)].astype(BF16)
        go(ytx1.at[t, :mid], yrx1.at[t, 0], s_y1.at[t, 0], r_y1.at[t, 0], up)
        go(ytx1.at[t, mid:], yrx1.at[t, 1], s_y1.at[t, 1], r_y1.at[t, 1], down)

    def y_relay_sum(t):
        above, below = lax.rem(y + 1, NY), lax.rem(y + NY - 1, NY)
        landed(yrx1.at[t, 0], r_y1.at[t, 0])
        ytx2[t, 0, :mid] = (part[t, above, :mid] + yrx1[t, 0].astype(F32)).astype(BF16)
        ytx2[t, 0, mid:] = part[t, above, mid:].astype(BF16)
        go(ytx2.at[t, 0], yrx2.at[t, 0], s_y2.at[t, 0], r_y2.at[t, 0], up)
        landed(yrx1.at[t, 1], r_y1.at[t, 1])
        ytx2[t, 1, :mid] = part[t, below, :mid].astype(BF16)
        ytx2[t, 1, mid:] = (part[t, below, mid:] + yrx1[t, 1].astype(F32)).astype(BF16)
        go(ytx2.at[t, 1], yrx2.at[t, 1], s_y2.at[t, 1], r_y2.at[t, 1], down)

    def z_copy(t, d):
        to = lax.rem(z + d, nz)
        return copy(ztx.at[t, to], zrx.at[t, d], s_z.at[t, d], r_z.at[t, d], at(y, z + d, core))

    def y_sum(t):
        landed(yrx2.at[t, 0], r_y2.at[t, 0])
        landed(yrx2.at[t, 1], r_y2.at[t, 1])
        total = part[t, y] + yrx2[t, 0].astype(F32) + yrx2[t, 1].astype(F32)
        ztx[t] = total.reshape(nz, seg, cols).astype(BF16)

        def send(d, carry):
            z_copy(t, d).start()
            return carry

        lax.fori_loop(1, nz, send, 0)

    def g_copy(t, d):
        mine = xt.at[t, y, pl.ds(pl.multiple_of(core * half + z * seg, seg), seg), :]
        return copy(mine, mine, s_gz.at[t, d], r_gz.at[t, d], at(y, z + d, core))

    def z_sum(t):
        def add(d, total):
            landed(zrx.at[t, d], r_z.at[t, d])
            return total + zrx[t, d].astype(F32)

        total = lax.fori_loop(1, nz, add, ztx[t, z].astype(F32))
        xt[t, y, pl.ds(pl.multiple_of(core * half + z * seg, seg), seg), :] = total.astype(BF16)

        def send(d, carry):
            g_copy(t, d).start()
            return carry

        lax.fori_loop(1, nz, send, 0)

    def half_of(t, y_, start, size):
        first = pl.multiple_of(core * half + start, mid)
        return xt.at[t, lax.rem(y_ + NY, NY), pl.ds(first, size), :]

    def z_gather(t):
        def wait(d, carry):
            g_copy(t, d).wait_recv()
            return carry

        lax.fori_loop(1, nz, wait, 0)
        mine = half_of(t, y, 0, half)
        go(mine, mine, s_gy.at[t, 0], r_gy.at[t, 0], up)
        go(mine, mine, s_gy.at[t, 1], r_gy.at[t, 1], down)
        go(mine, mine, s_gs.at[t, 0], r_gs.at[t, 0], sib)

    def y_gather(t):
        landed(half_of(t, y - 1, 0, half), r_gy.at[t, 0])
        piece = half_of(t, y - 1, 0, mid)
        go(piece, piece, s_gy.at[t, 2], r_gy.at[t, 2], up)
        landed(half_of(t, y + 1, 0, half), r_gy.at[t, 1])
        piece = half_of(t, y + 1, mid, mid)
        go(piece, piece, s_gy.at[t, 3], r_gy.at[t, 3], down)
        for k, d in ((1, -1), (2, 1)):
            piece = half_of(t, y + d, 0, half)
            go(piece, piece, s_gs.at[t, k], r_gs.at[t, k], sib)

    def y_relay_gather(t):
        landed(half_of(t, y + 2, 0, mid), r_gy.at[t, 2])
        landed(half_of(t, y + 2, mid, mid), r_gy.at[t, 3])
        piece = half_of(t, y + 2, 0, half)
        go(piece, piece, s_gs.at[t, 3], r_gs.at[t, 3], sib)

    def block_product(t):
        for k in range(4):
            landed(half_of(t, y, 0, half), r_gs.at[t, k])

        def block(b, carry):
            got = jnp.dot(
                xt[t, b], f_ref[pl.ds(pl.multiple_of(b * cols, cols), cols), :],
                preferred_element_type=F32,
            )
            acc[t // 3] = jnp.where(b == 0, got, acc[t // 3] + got)
            return carry

        if t == 3:
            landed(relay.at[0], r_p.at[2])
            go(relay.at[0], prx.at[2, :half], s_p.at[4], r_p.at[4], right)
            landed(relay.at[1], r_p.at[3])
            go(relay.at[1], prx.at[2, half:], s_p.at[5], r_p.at[5], left)
        lax.fori_loop(0, NY, block, 0)
        if t < 3:
            ptx[t] = acc[0].astype(BF16)
        if t == 0:
            go(ptx.at[0], prx.at[1], s_p.at[1], r_p.at[1], left)
        if t == 1:
            go(ptx.at[1], prx.at[0], s_p.at[0], r_p.at[0], right)
        if t == 2:
            go(ptx.at[2, :half], relay.at[0], s_p.at[2], r_p.at[2], right)
            go(ptx.at[2, half:], relay.at[1], s_p.at[3], r_p.at[3], left)

    stages = (
        weights_product, core_sum, y_relay_sum, y_sum, z_sum, z_gather, y_gather, y_relay_gather, block_product,
    )
    for step in range(len(stages) + nx - 1):
        for k in reversed(range(len(stages))):
            if 0 <= step - k < nx:
                stages[k](step - k)

    landed(prx.at[0], r_p.at[0])
    landed(prx.at[1], r_p.at[1])
    for h in range(2):
        piece = slice(h * half, (h + 1) * half)
        landed(prx.at[2, piece], r_p.at[4 + h])
        total = acc[1, piece]
        for source in range(3):
            total = total + prx[source, piece].astype(F32)
        blocks = [
            total[a * thin : (a + 1) * thin, c * width : (c + 1) * width][None]
            for a in range(virt)
            for c in range(virt)
        ]
        flat = jnp.concatenate(blocks, axis=0).reshape(virt * virt, thin * width).astype(BF16)
        for r in range(CAP):
            chosen = picks_ref[:, r, :][:, : virt * virt].astype(BF16)
            got = jnp.dot(chosen, flat, preferred_element_type=F32)
            bsend[h, :, r] = got.reshape(n, thin, width).astype(BF16)
        each_peer(lambda d, h=h: back_copy(h, d).start())
        bgot[h, pair] = bsend[h, pair]

    count = out_ref.shape[0]
    few = count // 2

    def spot(who, h, first_block):
        low = lax.rem(who + nx, nx) * (2 * thin) + h * thin
        return out_ref.at[pl.ds(first_block, few), pl.ds(pl.multiple_of(low, thin), thin), :]

    for h in range(2):
        each_peer(lambda d, h=h: back_copy(h, d).wait_recv())
        total = 0.0
        for r in range(CAP):
            rows_r = bgot[h, :, r].astype(F32).reshape(n, thin * width).astype(BF16)
            total = total + jnp.dot(place_ref[r], rows_r, preferred_element_type=F32)
        low = pl.multiple_of(aux * (2 * thin) + h * thin, thin)
        out_ref[:, pl.ds(low, thin), :] = total.reshape(count, thin, width).astype(BF16)
        for q, to in enumerate((right, left)):
            for b in range(2):
                mine = spot(aux, h, (b ^ q) * few)
                m = 2 * q + b
                go(mine, mine, s_j.at[h, m], r_j.at[h, m], to)
    for h in range(2):
        from_left, from_right = spot(aux - 1, h, 0), spot(aux + 1, h, few)
        landed(from_left, r_j.at[h, 0])
        go(from_left, from_left, s_j.at[h, 4], r_j.at[h, 4], right)
        landed(from_right, r_j.at[h, 2])
        go(from_right, from_right, s_j.at[h, 5], r_j.at[h, 5], left)
    for h in range(2):
        landed(spot(aux - 1, h, few), r_j.at[h, 1])
        landed(spot(aux + 1, h, 0), r_j.at[h, 3])
        landed(spot(aux + 2, h, 0), r_j.at[h, 4])
        landed(spot(aux + 2, h, few), r_j.at[h, 5])

    def drained(d):
        meta_copy(d).wait_send()
        for h in range(2):
            out_copy(h, d).wait_send()
            back_copy(h, d).wait_send()

    each_peer(drained)
    for c in sent:
        c.wait_send()
    for t in range(nx):
        def drain(d, carry, t=t):
            z_copy(t, d).wait_send()
            g_copy(t, d).wait_send()
            return carry

        lax.fori_loop(1, nz, drain, 0)


def cycle(factors, send, meta, place):
    n, _, part, width = send.shape
    nx = lax.axis_size("aux")
    nz = n // (2 * NY)
    share_rows, virt, _ = factors.shape
    rows, flat = virt * part, virt * width
    half, cols = rows // 2, share_rows // NY
    seg, mid, thin = half // nz, half // 2, part // 2
    dma = pltpu.SemaphoreType.DMA
    vmem = pl.BlockSpec(memory_space=pltpu.VMEM)
    pairs = [
        (n,), (2, n), (2, n), (2, 6), (6,), (nx,), (nx, 2), (nx, 2), (nx, nz), (nx, nz), (nx, 4),
        (nx, 4), (6,),
    ]
    return pl.pallas_call(
        functools.partial(cycle_kernel, nz, nx),
        out_shape=jax.ShapeDtypeStruct((place.shape[1], nx * part, width), BF16),
        in_specs=[vmem] * 4,
        out_specs=vmem,
        scratch_shapes=[
            pltpu.VMEM((share_rows, flat), BF16),
            pltpu.VMEM((2, n, CAP, thin, width), BF16),
            pltpu.VMEM(meta.shape, F32),
            pltpu.VMEM((2, n, CAP, thin, width), BF16),
            pltpu.VMEM((2, n, CAP, thin, width), BF16),
            pltpu.VMEM((rows, flat), BF16),
            pltpu.VMEM((3, rows, flat), BF16),
            pltpu.VMEM((nx, NY, half, cols), F32),
            pltpu.VMEM((nx, NY, half, cols), F32),
            pltpu.VMEM((nx, NY, half, cols), F32),
            pltpu.VMEM((nx, half, cols), BF16),
            pltpu.VMEM((nx, 2, mid, cols), BF16),
            pltpu.VMEM((nx, 2, half, cols), BF16),
            pltpu.VMEM((nx, 2, half, cols), BF16),
            pltpu.VMEM((nx, nz, seg, cols), BF16),
            pltpu.VMEM((nx, nz, seg, cols), BF16),
            pltpu.VMEM((nx, NY, rows, cols), BF16),
            pltpu.VMEM((3, rows, flat), BF16),
            pltpu.VMEM((3, rows, flat), BF16),
            pltpu.VMEM((2, half, flat), BF16),
            pltpu.VMEM((2, rows, flat), F32),
        ]
        + [dma(shape) for shape in pairs for _ in range(2)],
        compiler_params=pltpu.CompilerParams(
            collective_id=0, has_side_effects=True, vmem_limit_bytes=58 << 20
        ),
        cost_estimate=pl.CostEstimate(
            flops=4 * nx * rows * flat * share_rows, bytes_accessed=8 << 20, transcendentals=0
        ),
    )(factors, send, meta, place)


def on_device(factors, amplitudes, block_list, owner_map):
    pair_count = lax.axis_size("pair")
    aux_count = lax.axis_size("aux")
    share = lax.axis_index("aux")
    block_count, block_width, _ = amplitudes.shape
    virt = factors.shape[2]
    lanes = max(128, virt * virt)
    part = block_width // aux_count
    ids = lax.iota(jnp.int32, block_count)
    hits = block_list[:, 0][:, None] == lax.iota(jnp.int32, owner_map.shape[0])[None, :]
    owners = jnp.sum(jnp.where(hits, owner_map[None, :], 0), axis=1)
    combo = block_list[:, 1] * virt + block_list[:, 2]
    same = (owners[:, None] == owners[None, :]) & (ids[None, :] < ids[:, None])
    rank = jnp.sum(same.astype(jnp.int32), axis=1)
    slots = owners * CAP + rank
    placing = (slots[:, None] == lax.iota(jnp.int32, pair_count * CAP)[None, :]).astype(BF16)
    at_combo = (combo[:, None] == lax.iota(jnp.int32, lanes)[None, :]).astype(BF16)
    meta = jnp.einsum("js,jn->sn", placing, at_combo, preferred_element_type=F32)
    mine = lax.dynamic_slice_in_dim(amplitudes, share * part, part, axis=1)
    sent = jnp.einsum("js,jm->sm", placing, mine.reshape(block_count, -1), preferred_element_type=F32)
    to_owner = owners[:, None] == lax.iota(jnp.int32, pair_count)[None, :]
    place = jnp.stack([to_owner & (rank == r)[:, None] for r in range(CAP)]).astype(BF16)
    return cycle(
        factors.reshape(-1, virt, block_width),
        sent.astype(BF16).reshape(pair_count, CAP, part, block_width),
        meta.reshape(pair_count, CAP, lanes),
        place,
    )


def solution(mesh):
    placed = (P("pair", "aux", None, None), P("pair", None, None), P("pair", None), P())
    return jax.shard_map(
        on_device, mesh=mesh, in_specs=placed, out_specs=P("pair", None, None), check_vma=False
    )
```

```python
import functools

import jax
import jax.numpy as jnp
from jax import lax
from jax.experimental import pallas as pl
from jax.experimental.pallas import tpu as pltpu
from jax.sharding import PartitionSpec as P

CAP = 2
NY = 4
F32 = jnp.float32
BF16 = jnp.bfloat16
MESH = pl.DeviceIdType.MESH
NT = (((1,), (1,)), ((), ()))
TN = (((0,), (0,)), ((), ()))


def cycle_kernel(
    nz, nx, factor_ref, send_ref, meta_ref, place_ref, out_ref, f_ref, got_ref, picks_ref, bsend,
    bgot, w_ref, wall, sibtx, sibrx, part, ytx1, yrx1, ytx2, yrx2, ztx, zrx, xt, ptx, prx, relay,
    acc, s_m, r_m, s_a, r_a, s_b, r_b, s_j, r_j, s_w, r_w, s_sib, r_sib, s_y1, r_y1, s_y2, r_y2,
    s_z, r_z, s_gz, r_gz, s_gy, r_gy, s_gs, r_gs, s_p, r_p,
):
    pair, aux = lax.axis_index("pair"), lax.axis_index("aux")
    core, z, y = lax.rem(pair, 2), lax.rem(pair // 2, nz), pair // (2 * nz)
    half = sibtx.shape[2]
    seg = half // nz
    mid = half // 2
    cols = part.shape[3]
    rows = 2 * half

    def at(y_, z_, c_):
        return {"pair": (lax.rem(y_ + NY, NY) * nz + lax.rem(z_ + nz, nz)) * 2 + c_}

    sib = at(y, z, 1 - core)
    up, down = at(y + 1, z, core), at(y - 1, z, core)
    right, left = {"aux": lax.rem(aux + 1, nx)}, {"aux": lax.rem(aux + nx - 1, nx)}

    def copy(src, dst, send, recv, to):
        return pltpu.make_async_remote_copy(
            src_ref=src, dst_ref=dst, send_sem=send, recv_sem=recv, device_id=to, device_id_type=MESH
        )

    n = 2 * NY * nz
    barrier = pltpu.get_barrier_semaphore()
    for peer in (right, left):
        pl.semaphore_signal(barrier, inc=1, device_id=peer, device_id_type=MESH)

    def peer_at(d):
        return lax.rem(pair + d, n)

    def greet(d, carry):
        pl.semaphore_signal(
            barrier, inc=1, device_id={"pair": peer_at(d)}, device_id_type=MESH
        )
        return carry

    lax.fori_loop(1, n, greet, 0)
    pl.semaphore_wait(barrier, n + 1)

    sent = []

    def go(*args):
        c = copy(*args)
        c.start()
        sent.append(c)
        return c

    def landed(dst, recv):
        copy(dst, dst, recv, recv, sib).wait_recv()

    thin = send_ref.shape[2] // 2
    width = send_ref.shape[3]
    virt = w_ref.shape[1] // width

    def meta_copy(d):
        to = peer_at(d)
        return copy(
            meta_ref.at[to], picks_ref.at[pair], s_m.at[0], r_m.at[0], {"pair": to}
        )

    def out_copy(h, d):
        to = peer_at(d)
        return copy(
            send_ref.at[to, :, h * thin : (h + 1) * thin, :], got_ref.at[h, pair], s_a.at[h],
            r_a.at[h], {"pair": to},
        )

    def back_copy(h, d):
        to = peer_at(d)
        return copy(bsend.at[h, to], bgot.at[h, pair], s_b.at[h], r_b.at[h], {"pair": to})

    def each_peer(act):
        def one(d, carry):
            act(d)
            return carry

        lax.fori_loop(1, n, one, 0)

    def first(d):
        meta_copy(d).start()
        out_copy(0, d).start()

    each_peer(first)
    each_peer(lambda d: out_copy(1, d).start())
    picks_ref[pair] = meta_ref[pair]
    for h in range(2):
        got_ref[h, pair] = send_ref[pair, :, h * thin : (h + 1) * thin, :]
    step = 64 if f_ref.shape[0] % 64 == 0 else f_ref.shape[0]

    def flatten(i, carry):
        at_rows = pl.ds(pl.multiple_of(i * step, step), step)
        f_ref[at_rows, :] = factor_ref[at_rows].astype(F32).reshape(step, -1).astype(BF16)
        return carry

    lax.fori_loop(0, f_ref.shape[0] // step, flatten, 0)

    def combine(h):
        total = 0.0
        for r in range(CAP):
            rows_r = got_ref[h, :, r].astype(F32).reshape(n, thin * width).astype(BF16)
            total = total + lax.dot_general(
                picks_ref[:, r, :].astype(BF16), rows_r, TN, preferred_element_type=F32
            )
        total = total[: virt * virt].reshape(virt * virt, thin, width).astype(BF16)
        for a in range(virt):
            for c in range(virt):
                low = h * half + a * thin
                w_ref[low : low + thin, c * width : (c + 1) * width] = total[a * virt + c]
        piece = slice(h * half, (h + 1) * half)
        go(w_ref.at[piece], wall.at[0, piece], s_w.at[2 * h], r_w.at[2 * h], right)
        go(w_ref.at[piece], wall.at[1, piece], s_w.at[2 * h + 1], r_w.at[2 * h + 1], left)

    landed(picks_ref.at[: n - 1], r_m.at[0])
    landed(got_ref.at[0, : n - 1], r_a.at[0])
    combine(0)
    landed(wall.at[0, :half], r_w.at[0])
    go(wall.at[0, :half], wall.at[2, :half], s_w.at[4], r_w.at[4], right)
    landed(got_ref.at[1, : n - 1], r_a.at[1])
    combine(1)

    own = pl.multiple_of(core * half, half)
    other = pl.multiple_of((1 - core) * half, half)

    def weights_product(t):
        if t == 0:
            landed(wall.at[1, half:], r_w.at[3])
            go(wall.at[1, half:], wall.at[2, half:], s_w.at[5], r_w.at[5], left)
            landed(wall.at[0, half:], r_w.at[2])
        if t == 1:
            landed(wall.at[1, :half], r_w.at[1])
        if t == 2:
            landed(wall.at[2, :half], r_w.at[4])
            landed(wall.at[2, half:], r_w.at[5])
        w = w_ref if t == 3 else wall.at[t]
        w_both = jnp.concatenate([w[pl.ds(other, half), :], w[pl.ds(own, half), :]], axis=0)

        def block(b, carry):
            got = lax.dot_general(
                w_both, f_ref[pl.ds(pl.multiple_of(b * cols, cols), cols), :], NT,
                preferred_element_type=F32,
            )
            sibtx[t, b] = got[:half]
            part[t, b] = got[half:]
            return carry

        lax.fori_loop(0, NY, block, 0)
        go(sibtx.at[t], sibrx.at[t], s_sib.at[t], r_sib.at[t], sib)

    def core_sum(t):
        landed(sibrx.at[t], r_sib.at[t])

        def block(b, carry):
            part[t, b] = part[t, b] + sibrx[t, b]
            return carry

        lax.fori_loop(0, NY, block, 0)
        ytx1[t] = part[t, lax.rem(y + 2, NY)].astype(BF16)
        go(ytx1.at[t, :mid], yrx1.at[t, 0], s_y1.at[t, 0], r_y1.at[t, 0], up)
        go(ytx1.at[t, mid:], yrx1.at[t, 1], s_y1.at[t, 1], r_y1.at[t, 1], down)

    def y_relay_sum(t):
        above, below = lax.rem(y + 1, NY), lax.rem(y + NY - 1, NY)
        landed(yrx1.at[t, 0], r_y1.at[t, 0])
        ytx2[t, 0, :mid] = (part[t, above, :mid] + yrx1[t, 0].astype(F32)).astype(BF16)
        ytx2[t, 0, mid:] = part[t, above, mid:].astype(BF16)
        go(ytx2.at[t, 0], yrx2.at[t, 0], s_y2.at[t, 0], r_y2.at[t, 0], up)
        landed(yrx1.at[t, 1], r_y1.at[t, 1])
        ytx2[t, 1, :mid] = part[t, below, :mid].astype(BF16)
        ytx2[t, 1, mid:] = (part[t, below, mid:] + yrx1[t, 1].astype(F32)).astype(BF16)
        go(ytx2.at[t, 1], yrx2.at[t, 1], s_y2.at[t, 1], r_y2.at[t, 1], down)

    def z_copy(t, d):
        to = lax.rem(z + d, nz)
        return copy(ztx.at[t, to], zrx.at[t, d], s_z.at[t], r_z.at[t], at(y, z + d, core))

    def y_sum(t):
        landed(yrx2.at[t, 0], r_y2.at[t, 0])
        landed(yrx2.at[t, 1], r_y2.at[t, 1])
        total = part[t, y] + yrx2[t, 0].astype(F32) + yrx2[t, 1].astype(F32)
        ztx[t] = total.reshape(nz, seg, cols).astype(BF16)

        def send(d, carry):
            z_copy(t, d).start()
            return carry

        lax.fori_loop(1, nz, send, 0)

    def g_copy(t, d):
        mine = xt.at[t, y, pl.ds(pl.multiple_of(core * half + z * seg, seg), seg), :]
        return copy(mine, mine, s_gz.at[t], r_gz.at[t], at(y, z + d, core))

    def z_sum(t):
        landed(zrx.at[t, 1:], r_z.at[t])

        def add(d, total):
            return total + zrx[t, d].astype(F32)

        total = lax.fori_loop(1, nz, add, ztx[t, z].astype(F32))
        xt[t, y, pl.ds(pl.multiple_of(core * half + z * seg, seg), seg), :] = total.astype(BF16)

        def send(d, carry):
            g_copy(t, d).start()
            return carry

        lax.fori_loop(1, nz, send, 0)

    def half_of(t, y_, start, size):
        first = pl.multiple_of(core * half + start, mid)
        return xt.at[t, lax.rem(y_ + NY, NY), pl.ds(first, size), :]

    def z_gather(t):
        landed(zrx.at[t, 1:], r_gz.at[t])
        mine = half_of(t, y, 0, half)
        go(mine, mine, s_gy.at[t, 0], r_gy.at[t, 0], up)
        go(mine, mine, s_gy.at[t, 1], r_gy.at[t, 1], down)
        go(mine, mine, s_gs.at[t, 0], r_gs.at[t, 0], sib)

    def y_gather(t):
        landed(half_of(t, y - 1, 0, half), r_gy.at[t, 0])
        piece = half_of(t, y - 1, 0, mid)
        go(piece, piece, s_gy.at[t, 2], r_gy.at[t, 2], up)
        landed(half_of(t, y + 1, 0, half), r_gy.at[t, 1])
        piece = half_of(t, y + 1, mid, mid)
        go(piece, piece, s_gy.at[t, 3], r_gy.at[t, 3], down)
        for k, d in ((1, -1), (2, 1)):
            piece = half_of(t, y + d, 0, half)
            go(piece, piece, s_gs.at[t, k], r_gs.at[t, k], sib)

    def y_relay_gather(t):
        landed(half_of(t, y + 2, 0, mid), r_gy.at[t, 2])
        landed(half_of(t, y + 2, mid, mid), r_gy.at[t, 3])
        piece = half_of(t, y + 2, 0, half)
        go(piece, piece, s_gs.at[t, 3], r_gs.at[t, 3], sib)

    def block_product(t):
        for k in range(4):
            landed(half_of(t, y, 0, half), r_gs.at[t, k])

        def block(b, carry):
            got = jnp.dot(
                xt[t, b], f_ref[pl.ds(pl.multiple_of(b * cols, cols), cols), :],
                preferred_element_type=F32,
            )
            acc[t // 3] = jnp.where(b == 0, got, acc[t // 3] + got)
            return carry

        if t == 3:
            landed(relay.at[0], r_p.at[2])
            go(relay.at[0], prx.at[2, :half], s_p.at[4], r_p.at[4], right)
            landed(relay.at[1], r_p.at[3])
            go(relay.at[1], prx.at[2, half:], s_p.at[5], r_p.at[5], left)
        lax.fori_loop(0, NY, block, 0)
        if t < 3:
            ptx[t] = acc[0].astype(BF16)
        if t == 0:
            go(ptx.at[0], prx.at[1], s_p.at[1], r_p.at[1], left)
        if t == 1:
            go(ptx.at[1], prx.at[0], s_p.at[0], r_p.at[0], right)
        if t == 2:
            go(ptx.at[2, :half], relay.at[0], s_p.at[2], r_p.at[2], right)
            go(ptx.at[2, half:], relay.at[1], s_p.at[3], r_p.at[3], left)

    stages = (
        weights_product, core_sum, y_relay_sum, y_sum, z_sum, z_gather, y_gather, y_relay_gather, block_product,
    )
    for step in range(len(stages) + nx - 1):
        for k in reversed(range(len(stages))):
            if 0 <= step - k < nx:
                stages[k](step - k)

    landed(prx.at[0], r_p.at[0])
    landed(prx.at[1], r_p.at[1])
    for h in range(2):
        piece = slice(h * half, (h + 1) * half)
        landed(prx.at[2, piece], r_p.at[4 + h])
        total = acc[1, piece]
        for source in range(3):
            total = total + prx[source, piece].astype(F32)
        blocks = [
            total[a * thin : (a + 1) * thin, c * width : (c + 1) * width][None]
            for a in range(virt)
            for c in range(virt)
        ]
        flat = jnp.concatenate(blocks, axis=0).reshape(virt * virt, thin * width).astype(BF16)
        for r in range(CAP):
            chosen = picks_ref[:, r, :][:, : virt * virt].astype(BF16)
            got = jnp.dot(chosen, flat, preferred_element_type=F32)
            bsend[h, :, r] = got.reshape(n, thin, width).astype(BF16)
        each_peer(lambda d, h=h: back_copy(h, d).start())
        bgot[h, pair] = bsend[h, pair]

    count = out_ref.shape[0]
    few = count // 2

    def spot(who, h, first_block):
        low = lax.rem(who + nx, nx) * (2 * thin) + h * thin
        return out_ref.at[pl.ds(first_block, few), pl.ds(pl.multiple_of(low, thin), thin), :]

    for h in range(2):
        landed(bgot.at[h, : n - 1], r_b.at[h])
        total = 0.0
        for r in range(CAP):
            rows_r = bgot[h, :, r].astype(F32).reshape(n, thin * width).astype(BF16)
            total = total + jnp.dot(place_ref[r], rows_r, preferred_element_type=F32)
        low = pl.multiple_of(aux * (2 * thin) + h * thin, thin)
        out_ref[:, pl.ds(low, thin), :] = total.reshape(count, thin, width).astype(BF16)
        for q, to in enumerate((right, left)):
            for b in range(2):
                mine = spot(aux, h, (b ^ q) * few)
                m = 2 * q + b
                go(mine, mine, s_j.at[h, m], r_j.at[h, m], to)
    for h in range(2):
        from_left, from_right = spot(aux - 1, h, 0), spot(aux + 1, h, few)
        landed(from_left, r_j.at[h, 0])
        go(from_left, from_left, s_j.at[h, 4], r_j.at[h, 4], right)
        landed(from_right, r_j.at[h, 2])
        go(from_right, from_right, s_j.at[h, 5], r_j.at[h, 5], left)
    for h in range(2):
        landed(spot(aux - 1, h, few), r_j.at[h, 1])
        landed(spot(aux + 1, h, 0), r_j.at[h, 3])
        landed(spot(aux + 2, h, 0), r_j.at[h, 4])
        landed(spot(aux + 2, h, few), r_j.at[h, 5])

    def left_here(src, send):
        copy(src, src, send, send, sib).wait_send()

    left_here(picks_ref.at[: n - 1], s_m.at[0])
    for h in range(2):
        left_here(got_ref.at[h, : n - 1], s_a.at[h])
        left_here(bgot.at[h, : n - 1], s_b.at[h])
    for c in sent:
        c.wait_send()
    for t in range(nx):
        left_here(zrx.at[t, 1:], s_z.at[t])
        left_here(zrx.at[t, 1:], s_gz.at[t])


def cycle(factors, send, meta, place):
    n, _, part, width = send.shape
    nx = lax.axis_size("aux")
    nz = n // (2 * NY)
    share_rows, virt, _ = factors.shape
    rows, flat = virt * part, virt * width
    half, cols = rows // 2, share_rows // NY
    seg, mid, thin = half // nz, half // 2, part // 2
    dma = pltpu.SemaphoreType.DMA
    vmem = pl.BlockSpec(memory_space=pltpu.VMEM)
    pairs = [
        (1,), (2,), (2,), (2, 6), (6,), (nx,), (nx, 2), (nx, 2), (nx,), (nx,), (nx, 4), (nx, 4),
        (6,),
    ]
    return pl.pallas_call(
        functools.partial(cycle_kernel, nz, nx),
        out_shape=jax.ShapeDtypeStruct((place.shape[1], nx * part, width), BF16),
        in_specs=[vmem] * 4,
        out_specs=vmem,
        scratch_shapes=[
            pltpu.VMEM((share_rows, flat), BF16),
            pltpu.VMEM((2, n, CAP, thin, width), BF16),
            pltpu.VMEM(meta.shape, F32),
            pltpu.VMEM((2, n, CAP, thin, width), BF16),
            pltpu.VMEM((2, n, CAP, thin, width), BF16),
            pltpu.VMEM((rows, flat), BF16),
            pltpu.VMEM((3, rows, flat), BF16),
            pltpu.VMEM((nx, NY, half, cols), F32),
            pltpu.VMEM((nx, NY, half, cols), F32),
            pltpu.VMEM((nx, NY, half, cols), F32),
            pltpu.VMEM((nx, half, cols), BF16),
            pltpu.VMEM((nx, 2, mid, cols), BF16),
            pltpu.VMEM((nx, 2, half, cols), BF16),
            pltpu.VMEM((nx, 2, half, cols), BF16),
            pltpu.VMEM((nx, nz, seg, cols), BF16),
            pltpu.VMEM((nx, nz, seg, cols), BF16),
            pltpu.VMEM((nx, NY, rows, cols), BF16),
            pltpu.VMEM((3, rows, flat), BF16),
            pltpu.VMEM((3, rows, flat), BF16),
            pltpu.VMEM((2, half, flat), BF16),
            pltpu.VMEM((2, rows, flat), F32),
        ]
        + [dma(shape) for shape in pairs for _ in range(2)],
        compiler_params=pltpu.CompilerParams(
            collective_id=0, has_side_effects=True, vmem_limit_bytes=46 << 20
        ),
        cost_estimate=pl.CostEstimate(
            flops=4 * nx * rows * flat * share_rows, bytes_accessed=8 << 20, transcendentals=0
        ),
    )(factors, send, meta, place)


def on_device(factors, amplitudes, block_list, owner_map):
    pair_count = lax.axis_size("pair")
    aux_count = lax.axis_size("aux")
    share = lax.axis_index("aux")
    block_count, block_width, _ = amplitudes.shape
    virt = factors.shape[2]
    lanes = max(128, virt * virt)
    part = block_width // aux_count
    ids = lax.iota(jnp.int32, block_count)
    hits = block_list[:, 0][:, None] == lax.iota(jnp.int32, owner_map.shape[0])[None, :]
    owners = jnp.sum(jnp.where(hits, owner_map[None, :], 0), axis=1)
    combo = block_list[:, 1] * virt + block_list[:, 2]
    same = (owners[:, None] == owners[None, :]) & (ids[None, :] < ids[:, None])
    rank = jnp.sum(same.astype(jnp.int32), axis=1)
    slots = owners * CAP + rank
    placing = (slots[:, None] == lax.iota(jnp.int32, pair_count * CAP)[None, :]).astype(BF16)
    at_combo = (combo[:, None] == lax.iota(jnp.int32, lanes)[None, :]).astype(BF16)
    meta = jnp.einsum("js,jn->sn", placing, at_combo, preferred_element_type=F32)
    mine = lax.dynamic_slice_in_dim(amplitudes, share * part, part, axis=1)
    sent = jnp.einsum("js,jm->sm", placing, mine.reshape(block_count, -1), preferred_element_type=F32)
    to_owner = owners[:, None] == lax.iota(jnp.int32, pair_count)[None, :]
    place = jnp.stack([to_owner & (rank == r)[:, None] for r in range(CAP)]).astype(BF16)
    return cycle(
        factors.reshape(-1, virt, block_width),
        sent.astype(BF16).reshape(pair_count, CAP, part, block_width),
        meta.reshape(pair_count, CAP, lanes),
        place,
    )


def solution(mesh):
    placed = (P("pair", "aux", None, None), P("pair", None, None), P("pair", None), P())
    return jax.shard_map(
        on_device, mesh=mesh, in_specs=placed, out_specs=P("pair", None, None), check_vma=False
    )
```

```python
import functools

import jax
import jax.numpy as jnp
from jax import lax
from jax.experimental import pallas as pl
from jax.experimental.pallas import tpu as pltpu
from jax.sharding import PartitionSpec as P

CAP = 2
ORDER = ((3, 0), (0, 0), (1, 0), (2, 0), (0, 1), (1, 1), (2, 1), (3, 1))
NY = 4
F32 = jnp.float32
BF16 = jnp.bfloat16
MESH = pl.DeviceIdType.MESH
NT = (((1,), (1,)), ((), ()))
TN = (((0,), (0,)), ((), ()))


def cycle_kernel(
    nz, nx, factor_ref, send_ref, meta_ref, place_ref, out_ref, f_ref, got_ref, picks_ref, bsend,
    bgot, w_ref, wall, sibtx, sibrx, part, ytx1, yrx1, ytx2, yrx2, ztx, zrx, zg, xt, ptx, prx, relay,
    acc, s_m, r_m, s_a, r_a, s_b, r_b, s_j, r_j, s_w, r_w, s_sib, r_sib, s_y1, r_y1, s_y2, r_y2,
    s_z, r_z, s_gz, r_gz, s_gy, r_gy, s_gs, r_gs, s_p, r_p,
):
    pair, aux = lax.axis_index("pair"), lax.axis_index("aux")
    core, z, y = lax.rem(pair, 2), lax.rem(pair // 2, nz), pair // (2 * nz)
    half = sibtx.shape[2]
    seg = half // nz
    mid = half // 2
    cols = part.shape[3]
    rows = 2 * half
    chunks = len(ORDER)

    def at(y_, z_, c_):
        return {"pair": (lax.rem(y_ + NY, NY) * nz + lax.rem(z_ + nz, nz)) * 2 + c_}

    sib = at(y, z, 1 - core)
    up, down = at(y + 1, z, core), at(y - 1, z, core)
    right, left = {"aux": lax.rem(aux + 1, nx)}, {"aux": lax.rem(aux + nx - 1, nx)}

    def copy(src, dst, send, recv, to):
        return pltpu.make_async_remote_copy(
            src_ref=src, dst_ref=dst, send_sem=send, recv_sem=recv, device_id=to, device_id_type=MESH
        )

    n = 2 * NY * nz
    barrier = pltpu.get_barrier_semaphore()
    for peer in (right, left):
        pl.semaphore_signal(barrier, inc=1, device_id=peer, device_id_type=MESH)

    def peer_at(d):
        return lax.rem(pair + d, n)

    def greet(d, carry):
        pl.semaphore_signal(
            barrier, inc=1, device_id={"pair": peer_at(d)}, device_id_type=MESH
        )
        return carry

    lax.fori_loop(1, n, greet, 0)
    pl.semaphore_wait(barrier, n + 1)

    sent = []

    def go(*args):
        c = copy(*args)
        c.start()
        sent.append(c)
        return c

    def landed(dst, recv):
        copy(dst, dst, recv, recv, sib).wait_recv()

    thin = send_ref.shape[2] // 2
    width = send_ref.shape[3]
    virt = w_ref.shape[1] // width

    def meta_copy(d):
        to = peer_at(d)
        return copy(
            meta_ref.at[to], picks_ref.at[pair], s_m.at[0], r_m.at[0], {"pair": to}
        )

    def out_copy(h, d):
        to = peer_at(d)
        return copy(
            send_ref.at[to, :, h * thin : (h + 1) * thin, :], got_ref.at[h, pair], s_a.at[h],
            r_a.at[h], {"pair": to},
        )

    def back_copy(h, d):
        to = peer_at(d)
        return copy(bsend.at[h, to], bgot.at[h, pair], s_b.at[h], r_b.at[h], {"pair": to})

    def each_peer(act):
        def one(d, carry):
            act(d)
            return carry

        lax.fori_loop(1, n, one, 0)

    def first(d):
        meta_copy(d).start()
        out_copy(0, d).start()

    each_peer(first)
    each_peer(lambda d: out_copy(1, d).start())
    picks_ref[pair] = meta_ref[pair]
    for h in range(2):
        got_ref[h, pair] = send_ref[pair, :, h * thin : (h + 1) * thin, :]
    step = 64 if f_ref.shape[0] % 64 == 0 else f_ref.shape[0]

    def flatten(i, carry):
        at_rows = pl.ds(pl.multiple_of(i * step, step), step)
        f_ref[at_rows, :] = factor_ref[at_rows].astype(F32).reshape(step, -1).astype(BF16)
        return carry

    lax.fori_loop(0, f_ref.shape[0] // step, flatten, 0)

    def combine(h):
        total = 0.0
        for r in range(CAP):
            rows_r = got_ref[h, :, r].astype(F32).reshape(n, thin * width).astype(BF16)
            total = total + lax.dot_general(
                picks_ref[:, r, :].astype(BF16), rows_r, TN, preferred_element_type=F32
            )
        total = total[: virt * virt].reshape(virt * virt, thin, width).astype(BF16)
        for a in range(virt):
            for c in range(virt):
                low = h * rows + a * thin
                w_ref[low : low + thin, c * width : (c + 1) * width] = total[a * virt + c]
        piece = slice(h * rows, (h + 1) * rows)
        go(w_ref.at[piece], wall.at[0, piece], s_w.at[h, 0], r_w.at[h, 0], right)
        go(w_ref.at[piece], wall.at[1, piece], s_w.at[h, 1], r_w.at[h, 1], left)

    landed(picks_ref.at[: n - 1], r_m.at[0])
    landed(got_ref.at[0, : n - 1], r_a.at[0])
    combine(0)

    own = pl.multiple_of(core * half, half)
    other = pl.multiple_of((1 - core) * half, half)

    def weights_product(t):
        share, h = ORDER[t]
        piece = slice(h * rows, (h + 1) * rows)
        low, high = slice(h * rows, h * rows + half), slice(h * rows + half, (h + 1) * rows)
        if share == 0:
            landed(wall.at[0, piece], r_w.at[h, 0])
            go(wall.at[0, low], wall.at[2, low], s_w.at[h, 2], r_w.at[h, 2], right)
            landed(wall.at[1, piece], r_w.at[h, 1])
            go(wall.at[1, high], wall.at[2, high], s_w.at[h, 3], r_w.at[h, 3], left)
        if share == 2:
            landed(wall.at[2, low], r_w.at[h, 2])
            landed(wall.at[2, high], r_w.at[h, 3])
        w = (w_ref if share == 3 else wall.at[share]).at[piece]
        w_both = jnp.concatenate([w[pl.ds(other, half), :], w[pl.ds(own, half), :]], axis=0)

        def block(b, carry):
            got = lax.dot_general(
                w_both, f_ref[pl.ds(pl.multiple_of(b * cols, cols), cols), :], NT,
                preferred_element_type=F32,
            )
            sibtx[t, b] = got[:half]
            part[t, b] = got[half:]
            return carry

        lax.fori_loop(0, NY, block, 0)
        go(sibtx.at[t], sibrx.at[t], s_sib.at[t], r_sib.at[t], sib)

    def core_sum(t):
        landed(sibrx.at[t], r_sib.at[t])

        def block(b, carry):
            part[t, b] = part[t, b] + sibrx[t, b]
            return carry

        lax.fori_loop(0, NY, block, 0)
        ytx1[t] = part[t, lax.rem(y + 2, NY)].astype(BF16)
        go(ytx1.at[t, :mid], yrx1.at[t, 0], s_y1.at[t, 0], r_y1.at[t, 0], up)
        go(ytx1.at[t, mid:], yrx1.at[t, 1], s_y1.at[t, 1], r_y1.at[t, 1], down)

    def y_relay_sum(t):
        above, below = lax.rem(y + 1, NY), lax.rem(y + NY - 1, NY)
        landed(yrx1.at[t, 0], r_y1.at[t, 0])
        ytx2[t, 0, :mid] = (part[t, above, :mid] + yrx1[t, 0].astype(F32)).astype(BF16)
        ytx2[t, 0, mid:] = part[t, above, mid:].astype(BF16)
        go(ytx2.at[t, 0], yrx2.at[t, 0], s_y2.at[t, 0], r_y2.at[t, 0], up)
        landed(yrx1.at[t, 1], r_y1.at[t, 1])
        ytx2[t, 1, :mid] = part[t, below, :mid].astype(BF16)
        ytx2[t, 1, mid:] = (part[t, below, mid:] + yrx1[t, 1].astype(F32)).astype(BF16)
        go(ytx2.at[t, 1], yrx2.at[t, 1], s_y2.at[t, 1], r_y2.at[t, 1], down)

    def z_copy(t, d):
        to = lax.rem(z + d, nz)
        return copy(ztx.at[t, to], zrx.at[t, d], s_z.at[t], r_z.at[t], at(y, z + d, core))

    def y_sum(t):
        landed(yrx2.at[t, 0], r_y2.at[t, 0])
        landed(yrx2.at[t, 1], r_y2.at[t, 1])
        total = part[t, y] + yrx2[t, 0].astype(F32) + yrx2[t, 1].astype(F32)
        ztx[t] = total.reshape(nz, seg, cols).astype(BF16)

        def send(d, carry):
            z_copy(t, d).start()
            return carry

        lax.fori_loop(1, nz, send, 0)

    def g_copy(t, d):
        mine = zg.at[t, z]
        return copy(mine, mine, s_gz.at[t], r_gz.at[t], at(y, z + d, core))

    def z_sum(t):
        landed(zrx.at[t, 1:], r_z.at[t])

        def add(d, total):
            return total + zrx[t, d].astype(F32)

        total = lax.fori_loop(1, nz, add, ztx[t, z].astype(F32))
        zg[t, z] = total.astype(BF16)

        def send(d, carry):
            g_copy(t, d).start()
            return carry

        lax.fori_loop(1, nz, send, 0)

    def half_of(t, y_, start, size):
        first = pl.multiple_of(core * half + start, mid)
        return xt.at[t, lax.rem(y_ + NY, NY), pl.ds(first, size), :]

    def z_gather(t):
        landed(zrx.at[t, 1:], r_gz.at[t])
        joined = zg[t].astype(F32).reshape(half, cols).astype(BF16)
        xt[t, y, pl.ds(pl.multiple_of(core * half, half), half), :] = joined
        mine = half_of(t, y, 0, half)
        go(mine, mine, s_gy.at[t, 0], r_gy.at[t, 0], up)
        go(mine, mine, s_gy.at[t, 1], r_gy.at[t, 1], down)
        go(mine, mine, s_gs.at[t, 0], r_gs.at[t, 0], sib)

    def y_gather(t):
        landed(half_of(t, y - 1, 0, half), r_gy.at[t, 0])
        piece = half_of(t, y - 1, 0, mid)
        go(piece, piece, s_gy.at[t, 2], r_gy.at[t, 2], up)
        landed(half_of(t, y + 1, 0, half), r_gy.at[t, 1])
        piece = half_of(t, y + 1, mid, mid)
        go(piece, piece, s_gy.at[t, 3], r_gy.at[t, 3], down)
        for k, d in ((1, -1), (2, 1)):
            piece = half_of(t, y + d, 0, half)
            go(piece, piece, s_gs.at[t, k], r_gs.at[t, k], sib)

    def y_relay_gather(t):
        landed(half_of(t, y + 2, 0, mid), r_gy.at[t, 2])
        landed(half_of(t, y + 2, mid, mid), r_gy.at[t, 3])
        piece = half_of(t, y + 2, 0, half)
        go(piece, piece, s_gs.at[t, 3], r_gs.at[t, 3], sib)

    def block_product(t):
        for k in range(4):
            landed(half_of(t, y, 0, half), r_gs.at[t, k])

        share, h = ORDER[t]
        piece = slice(h * rows, (h + 1) * rows)
        k = 1 + h if share == 3 else 0

        def block(b, carry):
            got = jnp.dot(
                xt[t, b], f_ref[pl.ds(pl.multiple_of(b * cols, cols), cols), :],
                preferred_element_type=F32,
            )
            acc[k] = jnp.where(b == 0, got, acc[k] + got)
            return carry

        if t and ORDER[t - 1][0] == 2:
            g = ORDER[t - 1][1]
            low, high = slice(g * rows, g * rows + half), slice(g * rows + half, (g + 1) * rows)
            landed(relay.at[g, 0], r_p.at[g, 2])
            go(relay.at[g, 0], prx.at[2, low], s_p.at[g, 4], r_p.at[g, 4], right)
            landed(relay.at[g, 1], r_p.at[g, 3])
            go(relay.at[g, 1], prx.at[2, high], s_p.at[g, 5], r_p.at[g, 5], left)
        lax.fori_loop(0, NY, block, 0)
        if share < 3:
            ptx[share, piece] = acc[0].astype(BF16)
        if share == 0:
            go(ptx.at[0, piece], prx.at[1, piece], s_p.at[h, 1], r_p.at[h, 1], left)
        if share == 1:
            go(ptx.at[1, piece], prx.at[0, piece], s_p.at[h, 0], r_p.at[h, 0], right)
        if share == 2:
            low, high = slice(h * rows, h * rows + half), slice(h * rows + half, (h + 1) * rows)
            go(ptx.at[2, low], relay.at[h, 0], s_p.at[h, 2], r_p.at[h, 2], right)
            go(ptx.at[2, high], relay.at[h, 1], s_p.at[h, 3], r_p.at[h, 3], left)

    stages = (
        weights_product, core_sum, y_relay_sum, y_sum, z_sum, z_gather, y_gather, y_relay_gather, block_product,
    )
    def give_back(h):
        piece = slice(h * rows, (h + 1) * rows)
        for k in (0, 1, 4, 5):
            landed(prx.at[min(k, 2), piece if k < 2 else slice(half)], r_p.at[h, k])
        total = acc[1 + h]
        for source in range(3):
            total = total + prx[source, piece].astype(F32)
        blocks = [
            total[a * thin : (a + 1) * thin, c * width : (c + 1) * width][None]
            for a in range(virt)
            for c in range(virt)
        ]
        flat = jnp.concatenate(blocks, axis=0).reshape(virt * virt, thin * width).astype(BF16)
        for r in range(CAP):
            chosen = picks_ref[:, r, :][:, : virt * virt].astype(BF16)
            got = jnp.dot(chosen, flat, preferred_element_type=F32)
            bsend[h, :, r] = got.reshape(n, thin, width).astype(BF16)
        each_peer(lambda d: back_copy(h, d).start())
        bgot[h, pair] = bsend[h, pair]

    for step in range(len(stages) + chunks - 1):
        if step == 3:
            landed(got_ref.at[1, : n - 1], r_a.at[1])
            combine(1)
        if step == 14:
            give_back(0)
        for k in reversed(range(len(stages))):
            if 0 <= step - k < chunks:
                stages[k](step - k)
    give_back(1)

    count = out_ref.shape[0]
    few = count // 2

    def spot(who, h, first_block):
        low = lax.rem(who + nx, nx) * (2 * thin) + h * thin
        return out_ref.at[pl.ds(first_block, few), pl.ds(pl.multiple_of(low, thin), thin), :]

    for h in range(2):
        landed(bgot.at[h, : n - 1], r_b.at[h])
        total = 0.0
        for r in range(CAP):
            rows_r = bgot[h, :, r].astype(F32).reshape(n, thin * width).astype(BF16)
            total = total + jnp.dot(place_ref[r], rows_r, preferred_element_type=F32)
        low = pl.multiple_of(aux * (2 * thin) + h * thin, thin)
        out_ref[:, pl.ds(low, thin), :] = total.reshape(count, thin, width).astype(BF16)
        for q, to in enumerate((right, left)):
            for b in range(2):
                mine = spot(aux, h, (b ^ q) * few)
                m = 2 * q + b
                go(mine, mine, s_j.at[h, m], r_j.at[h, m], to)
    for h in range(2):
        from_left, from_right = spot(aux - 1, h, 0), spot(aux + 1, h, few)
        landed(from_left, r_j.at[h, 0])
        go(from_left, from_left, s_j.at[h, 4], r_j.at[h, 4], right)
        landed(from_right, r_j.at[h, 2])
        go(from_right, from_right, s_j.at[h, 5], r_j.at[h, 5], left)
    for h in range(2):
        landed(spot(aux - 1, h, few), r_j.at[h, 1])
        landed(spot(aux + 1, h, 0), r_j.at[h, 3])
        landed(spot(aux + 2, h, 0), r_j.at[h, 4])
        landed(spot(aux + 2, h, few), r_j.at[h, 5])

    def left_here(src, send):
        copy(src, src, send, send, sib).wait_send()

    left_here(picks_ref.at[: n - 1], s_m.at[0])
    for h in range(2):
        left_here(got_ref.at[h, : n - 1], s_a.at[h])
        left_here(bgot.at[h, : n - 1], s_b.at[h])
    for c in sent:
        c.wait_send()
    for t in range(chunks):
        left_here(zrx.at[t, 1:], s_z.at[t])
        left_here(zrx.at[t, 1:], s_gz.at[t])


def cycle(factors, send, meta, place):
    n, _, part, width = send.shape
    nx = lax.axis_size("aux")
    nz = n // (2 * NY)
    share_rows, virt, _ = factors.shape
    rows, flat = virt * part, virt * width
    half, cols = rows // 4, share_rows // NY
    chunks = len(ORDER)
    seg, mid, thin = half // nz, half // 2, part // 2
    dma = pltpu.SemaphoreType.DMA
    vmem = pl.BlockSpec(memory_space=pltpu.VMEM)
    pairs = [
        (1,), (2,), (2,), (2, 6), (2, 4), (chunks,), (chunks, 2), (chunks, 2), (chunks,), (chunks,),
        (chunks, 4), (chunks, 4), (2, 6),
    ]
    return pl.pallas_call(
        functools.partial(cycle_kernel, nz, nx),
        out_shape=jax.ShapeDtypeStruct((place.shape[1], nx * part, width), BF16),
        in_specs=[vmem] * 4,
        out_specs=vmem,
        scratch_shapes=[
            pltpu.VMEM((share_rows, flat), BF16),
            pltpu.VMEM((2, n, CAP, thin, width), BF16),
            pltpu.VMEM(meta.shape, F32),
            pltpu.VMEM((2, n, CAP, thin, width), BF16),
            pltpu.VMEM((2, n, CAP, thin, width), BF16),
            pltpu.VMEM((rows, flat), BF16),
            pltpu.VMEM((3, rows, flat), BF16),
            pltpu.VMEM((chunks, NY, half, cols), F32),
            pltpu.VMEM((chunks, NY, half, cols), F32),
            pltpu.VMEM((chunks, NY, half, cols), F32),
            pltpu.VMEM((chunks, half, cols), BF16),
            pltpu.VMEM((chunks, 2, mid, cols), BF16),
            pltpu.VMEM((chunks, 2, half, cols), BF16),
            pltpu.VMEM((chunks, 2, half, cols), BF16),
            pltpu.VMEM((chunks, nz, seg, cols), BF16),
            pltpu.VMEM((chunks, nz, seg, cols), BF16),
            pltpu.VMEM((chunks, nz, seg, cols), BF16),
            pltpu.VMEM((chunks, NY, 2 * half, cols), BF16),
            pltpu.VMEM((3, rows, flat), BF16),
            pltpu.VMEM((3, rows, flat), BF16),
            pltpu.VMEM((2, 2, half, flat), BF16),
            pltpu.VMEM((3, 2 * half, flat), F32),
        ]
        + [dma(shape) for shape in pairs for _ in range(2)],
        compiler_params=pltpu.CompilerParams(
            collective_id=0, has_side_effects=True, vmem_limit_bytes=46 << 20
        ),
        cost_estimate=pl.CostEstimate(
            flops=4 * nx * rows * flat * share_rows, bytes_accessed=8 << 20, transcendentals=0
        ),
    )(factors, send, meta, place)


def on_device(factors, amplitudes, block_list, owner_map):
    pair_count = lax.axis_size("pair")
    aux_count = lax.axis_size("aux")
    share = lax.axis_index("aux")
    block_count, block_width, _ = amplitudes.shape
    virt = factors.shape[2]
    lanes = max(128, virt * virt)
    part = block_width // aux_count
    ids = lax.iota(jnp.int32, block_count)
    hits = block_list[:, 0][:, None] == lax.iota(jnp.int32, owner_map.shape[0])[None, :]
    owners = jnp.sum(jnp.where(hits, owner_map[None, :], 0), axis=1)
    combo = block_list[:, 1] * virt + block_list[:, 2]
    same = (owners[:, None] == owners[None, :]) & (ids[None, :] < ids[:, None])
    rank = jnp.sum(same.astype(jnp.int32), axis=1)
    slots = owners * CAP + rank
    placing = (slots[:, None] == lax.iota(jnp.int32, pair_count * CAP)[None, :]).astype(BF16)
    at_combo = (combo[:, None] == lax.iota(jnp.int32, lanes)[None, :]).astype(BF16)
    meta = jnp.einsum("js,jn->sn", placing, at_combo, preferred_element_type=F32)
    mine = lax.dynamic_slice_in_dim(amplitudes, share * part, part, axis=1)
    sent = jnp.einsum("js,jm->sm", placing, mine.reshape(block_count, -1), preferred_element_type=F32)
    to_owner = owners[:, None] == lax.iota(jnp.int32, pair_count)[None, :]
    place = jnp.stack([to_owner & (rank == r)[:, None] for r in range(CAP)]).astype(BF16)
    return cycle(
        factors.reshape(-1, virt, block_width),
        sent.astype(BF16).reshape(pair_count, CAP, part, block_width),
        meta.reshape(pair_count, CAP, lanes),
        place,
    )


def solution(mesh):
    placed = (P("pair", "aux", None, None), P("pair", None, None), P("pair", None), P())
    return jax.shard_map(
        on_device, mesh=mesh, in_specs=placed, out_specs=P("pair", None, None), check_vma=False
    )
```

```python
import functools

import jax
import jax.numpy as jnp
from jax import lax
from jax.experimental import pallas as pl
from jax.experimental.pallas import tpu as pltpu
from jax.sharding import PartitionSpec as P

CAP = 2
ORDER = ((3, 0), (0, 0), (1, 0), (2, 0), (0, 1), (1, 1), (2, 1), (3, 1))
NY = 4
F32 = jnp.float32
BF16 = jnp.bfloat16
MESH = pl.DeviceIdType.MESH
NT = (((1,), (1,)), ((), ()))
TN = (((0,), (0,)), ((), ()))


def cycle_kernel(
    nz, nx, factor_ref, send_ref, meta_ref, place_ref, out_ref, f_ref, got_ref, picks_ref, bsend,
    bgot, w_ref, wall, sibtx, sibrx, part, ytx, yrx, ztx, zrx, zg, xt, ptx, prx, relay,
    acc, s_m, r_m, s_a, r_a, s_b, r_b, s_j, r_j, s_w, r_w, s_sib, r_sib, s_y, r_y,
    s_z, r_z, s_gz, r_gz, s_gy, r_gy, s_gs, r_gs, s_p, r_p,
):
    pair, aux = lax.axis_index("pair"), lax.axis_index("aux")
    core, z, y = lax.rem(pair, 2), lax.rem(pair // 2, nz), pair // (2 * nz)
    half = sibtx.shape[2]
    seg = half // nz
    mid = half // 2
    cols = part.shape[3]
    rows = 2 * half
    chunks = len(ORDER)

    def at(y_, z_, c_):
        return {"pair": (lax.rem(y_ + NY, NY) * nz + lax.rem(z_ + nz, nz)) * 2 + c_}

    sib = at(y, z, 1 - core)
    up, down = at(y + 1, z, core), at(y - 1, z, core)
    right, left = {"aux": lax.rem(aux + 1, nx)}, {"aux": lax.rem(aux + nx - 1, nx)}

    def copy(src, dst, send, recv, to):
        return pltpu.make_async_remote_copy(
            src_ref=src, dst_ref=dst, send_sem=send, recv_sem=recv, device_id=to, device_id_type=MESH
        )

    n = 2 * NY * nz
    barrier = pltpu.get_barrier_semaphore()
    for peer in (right, left):
        pl.semaphore_signal(barrier, inc=1, device_id=peer, device_id_type=MESH)

    def peer_at(d):
        return lax.rem(pair + d, n)

    def greet(d, carry):
        pl.semaphore_signal(
            barrier, inc=1, device_id={"pair": peer_at(d)}, device_id_type=MESH
        )
        return carry

    lax.fori_loop(1, n, greet, 0)
    pl.semaphore_wait(barrier, n + 1)

    sent = []

    def go(*args):
        c = copy(*args)
        c.start()
        sent.append(c)
        return c

    def landed(dst, recv):
        copy(dst, dst, recv, recv, sib).wait_recv()

    thin = send_ref.shape[2] // 2
    width = send_ref.shape[3]
    virt = w_ref.shape[1] // width

    def meta_copy(d):
        to = peer_at(d)
        return copy(
            meta_ref.at[to], picks_ref.at[pair], s_m.at[0], r_m.at[0], {"pair": to}
        )

    def out_copy(h, d):
        to = peer_at(d)
        return copy(
            send_ref.at[to, :, h * thin : (h + 1) * thin, :], got_ref.at[h, pair], s_a.at[h],
            r_a.at[h], {"pair": to},
        )

    def back_copy(h, d):
        to = peer_at(d)
        return copy(bsend.at[h, to], bgot.at[h, pair], s_b.at[h], r_b.at[h], {"pair": to})

    def each_peer(act):
        def one(d, carry):
            act(d)
            return carry

        lax.fori_loop(1, n, one, 0)

    def first(d):
        meta_copy(d).start()
        out_copy(0, d).start()

    each_peer(first)
    each_peer(lambda d: out_copy(1, d).start())
    picks_ref[pair] = meta_ref[pair]
    for h in range(2):
        got_ref[h, pair] = send_ref[pair, :, h * thin : (h + 1) * thin, :]
    step = 64 if f_ref.shape[0] % 64 == 0 else f_ref.shape[0]

    def flatten(i, carry):
        at_rows = pl.ds(pl.multiple_of(i * step, step), step)
        f_ref[at_rows, :] = factor_ref[at_rows].astype(F32).reshape(step, -1).astype(BF16)
        return carry

    lax.fori_loop(0, f_ref.shape[0] // step, flatten, 0)

    def combine(h):
        total = 0.0
        for r in range(CAP):
            rows_r = got_ref[h, :, r].astype(F32).reshape(n, thin * width).astype(BF16)
            total = total + lax.dot_general(
                picks_ref[:, r, :].astype(BF16), rows_r, TN, preferred_element_type=F32
            )
        total = total[: virt * virt].reshape(virt * virt, thin, width).astype(BF16)
        for a in range(virt):
            for c in range(virt):
                low = h * rows + a * thin
                w_ref[low : low + thin, c * width : (c + 1) * width] = total[a * virt + c]
        piece = slice(h * rows, (h + 1) * rows)
        go(w_ref.at[piece], wall.at[0, piece], s_w.at[h, 0], r_w.at[h, 0], right)
        go(w_ref.at[piece], wall.at[1, piece], s_w.at[h, 1], r_w.at[h, 1], left)

    landed(picks_ref.at[: n - 1], r_m.at[0])
    landed(got_ref.at[0, : n - 1], r_a.at[0])
    combine(0)

    own = pl.multiple_of(core * half, half)
    other = pl.multiple_of((1 - core) * half, half)

    def weights_product(t):
        share, h = ORDER[t]
        piece = slice(h * rows, (h + 1) * rows)
        low, high = slice(h * rows, h * rows + half), slice(h * rows + half, (h + 1) * rows)
        if share == 0:
            landed(wall.at[0, piece], r_w.at[h, 0])
            go(wall.at[0, low], wall.at[2, low], s_w.at[h, 2], r_w.at[h, 2], right)
            landed(wall.at[1, piece], r_w.at[h, 1])
            go(wall.at[1, high], wall.at[2, high], s_w.at[h, 3], r_w.at[h, 3], left)
        if share == 2:
            landed(wall.at[2, low], r_w.at[h, 2])
            landed(wall.at[2, high], r_w.at[h, 3])
        w = (w_ref if share == 3 else wall.at[share]).at[piece]
        w_both = jnp.concatenate([w[pl.ds(other, half), :], w[pl.ds(own, half), :]], axis=0)

        def block(b, carry):
            got = lax.dot_general(
                w_both, f_ref[pl.ds(pl.multiple_of(b * cols, cols), cols), :], NT,
                preferred_element_type=F32,
            )
            sibtx[t, b] = got[:half]
            part[t, b] = got[half:]
            return carry

        lax.fori_loop(0, NY, block, 0)
        go(sibtx.at[t], sibrx.at[t], s_sib.at[t], r_sib.at[t], sib)

    def core_sum(t):
        landed(sibrx.at[t], r_sib.at[t])

        def block(b, carry):
            part[t, b] = part[t, b] + sibrx[t, b]
            return carry

        lax.fori_loop(0, NY, block, 0)
        for d in (2, 1, 3):
            ytx[t, d] = part[t, lax.rem(y + d, NY)].astype(BF16)
            go(ytx.at[t, d], yrx.at[t, d], s_y.at[t, d], r_y.at[t, d], at(y + d, z, core))

    def z_copy(t, d):
        to = lax.rem(z + d, nz)
        return copy(ztx.at[t, to], zrx.at[t, d], s_z.at[t], r_z.at[t], at(y, z + d, core))

    def y_sum(t):
        total = part[t, y]
        for d in (1, 3, 2):
            landed(yrx.at[t, d], r_y.at[t, d])
            total = total + yrx[t, d].astype(F32)
        ztx[t] = total.reshape(nz, seg, cols).astype(BF16)

        def send(d, carry):
            z_copy(t, d).start()
            return carry

        lax.fori_loop(1, nz, send, 0)

    def g_copy(t, d):
        mine = zg.at[t, z]
        return copy(mine, mine, s_gz.at[t], r_gz.at[t], at(y, z + d, core))

    def z_sum(t):
        landed(zrx.at[t, 1:], r_z.at[t])

        def add(d, total):
            return total + zrx[t, d].astype(F32)

        total = lax.fori_loop(1, nz, add, ztx[t, z].astype(F32))
        zg[t, z] = total.astype(BF16)

        def send(d, carry):
            g_copy(t, d).start()
            return carry

        lax.fori_loop(1, nz, send, 0)

    def half_of(t, y_, start, size):
        first = pl.multiple_of(core * half + start, mid)
        return xt.at[t, lax.rem(y_ + NY, NY), pl.ds(first, size), :]

    def z_gather(t):
        landed(zrx.at[t, 1:], r_gz.at[t])
        joined = zg[t].astype(F32).reshape(half, cols).astype(BF16)
        xt[t, y, pl.ds(pl.multiple_of(core * half, half), half), :] = joined
        mine = half_of(t, y, 0, half)
        for d in (2, 1, 3):
            go(mine, mine, s_gy.at[t, d], r_gy.at[t, d], at(y + d, z, core))
        go(mine, mine, s_gs.at[t, 0], r_gs.at[t, 0], sib)

    def y_gather(t):
        for d in (1, 3, 2):
            piece = half_of(t, y - d, 0, half)
            landed(piece, r_gy.at[t, d])
            go(piece, piece, s_gs.at[t, d], r_gs.at[t, d], sib)

    def block_product(t):
        for k in range(4):
            landed(half_of(t, y, 0, half), r_gs.at[t, k])

        share, h = ORDER[t]
        piece = slice(h * rows, (h + 1) * rows)
        k = 1 + h if share == 3 else 0

        def block(b, carry):
            got = jnp.dot(
                xt[t, b], f_ref[pl.ds(pl.multiple_of(b * cols, cols), cols), :],
                preferred_element_type=F32,
            )
            acc[k] = jnp.where(b == 0, got, acc[k] + got)
            return carry

        if t and ORDER[t - 1][0] == 2:
            g = ORDER[t - 1][1]
            low, high = slice(g * rows, g * rows + half), slice(g * rows + half, (g + 1) * rows)
            landed(relay.at[g, 0], r_p.at[g, 2])
            go(relay.at[g, 0], prx.at[2, low], s_p.at[g, 4], r_p.at[g, 4], right)
            landed(relay.at[g, 1], r_p.at[g, 3])
            go(relay.at[g, 1], prx.at[2, high], s_p.at[g, 5], r_p.at[g, 5], left)
        lax.fori_loop(0, NY, block, 0)
        if share < 3:
            ptx[share, piece] = acc[0].astype(BF16)
        if share == 0:
            go(ptx.at[0, piece], prx.at[1, piece], s_p.at[h, 1], r_p.at[h, 1], left)
        if share == 1:
            go(ptx.at[1, piece], prx.at[0, piece], s_p.at[h, 0], r_p.at[h, 0], right)
        if share == 2:
            low, high = slice(h * rows, h * rows + half), slice(h * rows + half, (h + 1) * rows)
            go(ptx.at[2, low], relay.at[h, 0], s_p.at[h, 2], r_p.at[h, 2], right)
            go(ptx.at[2, high], relay.at[h, 1], s_p.at[h, 3], r_p.at[h, 3], left)

    stages = (
        weights_product, core_sum, y_sum, z_sum, z_gather, y_gather, block_product,
    )
    def give_back(h):
        piece = slice(h * rows, (h + 1) * rows)
        for k in (0, 1, 4, 5):
            landed(prx.at[min(k, 2), piece if k < 2 else slice(half)], r_p.at[h, k])
        total = acc[1 + h]
        for source in range(3):
            total = total + prx[source, piece].astype(F32)
        blocks = [
            total[a * thin : (a + 1) * thin, c * width : (c + 1) * width][None]
            for a in range(virt)
            for c in range(virt)
        ]
        flat = jnp.concatenate(blocks, axis=0).reshape(virt * virt, thin * width).astype(BF16)
        for r in range(CAP):
            chosen = picks_ref[:, r, :][:, : virt * virt].astype(BF16)
            got = jnp.dot(chosen, flat, preferred_element_type=F32)
            bsend[h, :, r] = got.reshape(n, thin, width).astype(BF16)
        each_peer(lambda d: back_copy(h, d).start())
        bgot[h, pair] = bsend[h, pair]

    for step in range(len(stages) + chunks - 1):
        if step == 3:
            landed(got_ref.at[1, : n - 1], r_a.at[1])
            combine(1)
        if step == 12:
            give_back(0)
        for k in reversed(range(len(stages))):
            if 0 <= step - k < chunks:
                stages[k](step - k)
    give_back(1)

    count = out_ref.shape[0]
    few = count // 2

    def spot(who, h, first_block):
        low = lax.rem(who + nx, nx) * (2 * thin) + h * thin
        return out_ref.at[pl.ds(first_block, few), pl.ds(pl.multiple_of(low, thin), thin), :]

    for h in range(2):
        landed(bgot.at[h, : n - 1], r_b.at[h])
        total = 0.0
        for r in range(CAP):
            rows_r = bgot[h, :, r].astype(F32).reshape(n, thin * width).astype(BF16)
            total = total + jnp.dot(place_ref[r], rows_r, preferred_element_type=F32)
        low = pl.multiple_of(aux * (2 * thin) + h * thin, thin)
        out_ref[:, pl.ds(low, thin), :] = total.reshape(count, thin, width).astype(BF16)
        for q, to in enumerate((right, left)):
            for b in range(2):
                mine = spot(aux, h, (b ^ q) * few)
                m = 2 * q + b
                go(mine, mine, s_j.at[h, m], r_j.at[h, m], to)
    for h in range(2):
        from_left, from_right = spot(aux - 1, h, 0), spot(aux + 1, h, few)
        landed(from_left, r_j.at[h, 0])
        go(from_left, from_left, s_j.at[h, 4], r_j.at[h, 4], right)
        landed(from_right, r_j.at[h, 2])
        go(from_right, from_right, s_j.at[h, 5], r_j.at[h, 5], left)
    for h in range(2):
        landed(spot(aux - 1, h, few), r_j.at[h, 1])
        landed(spot(aux + 1, h, 0), r_j.at[h, 3])
        landed(spot(aux + 2, h, 0), r_j.at[h, 4])
        landed(spot(aux + 2, h, few), r_j.at[h, 5])

    def left_here(src, send):
        copy(src, src, send, send, sib).wait_send()

    left_here(picks_ref.at[: n - 1], s_m.at[0])
    for h in range(2):
        left_here(got_ref.at[h, : n - 1], s_a.at[h])
        left_here(bgot.at[h, : n - 1], s_b.at[h])
    for c in sent:
        c.wait_send()
    for t in range(chunks):
        left_here(zrx.at[t, 1:], s_z.at[t])
        left_here(zrx.at[t, 1:], s_gz.at[t])


def cycle(factors, send, meta, place):
    n, _, part, width = send.shape
    nx = lax.axis_size("aux")
    nz = n // (2 * NY)
    share_rows, virt, _ = factors.shape
    rows, flat = virt * part, virt * width
    half, cols = rows // 4, share_rows // NY
    chunks = len(ORDER)
    seg, mid, thin = half // nz, half // 2, part // 2
    dma = pltpu.SemaphoreType.DMA
    vmem = pl.BlockSpec(memory_space=pltpu.VMEM)
    pairs = [
        (1,), (2,), (2,), (2, 6), (2, 4), (chunks,), (chunks, NY), (chunks,), (chunks,),
        (chunks, 4), (chunks, 4), (2, 6),
    ]
    return pl.pallas_call(
        functools.partial(cycle_kernel, nz, nx),
        out_shape=jax.ShapeDtypeStruct((place.shape[1], nx * part, width), BF16),
        in_specs=[vmem] * 4,
        out_specs=vmem,
        scratch_shapes=[
            pltpu.VMEM((share_rows, flat), BF16),
            pltpu.VMEM((2, n, CAP, thin, width), BF16),
            pltpu.VMEM(meta.shape, F32),
            pltpu.VMEM((2, n, CAP, thin, width), BF16),
            pltpu.VMEM((2, n, CAP, thin, width), BF16),
            pltpu.VMEM((rows, flat), BF16),
            pltpu.VMEM((3, rows, flat), BF16),
            pltpu.VMEM((chunks, NY, half, cols), F32),
            pltpu.VMEM((chunks, NY, half, cols), F32),
            pltpu.VMEM((chunks, NY, half, cols), F32),
            pltpu.VMEM((chunks, NY, half, cols), BF16),
            pltpu.VMEM((chunks, NY, half, cols), BF16),
            pltpu.VMEM((chunks, nz, seg, cols), BF16),
            pltpu.VMEM((chunks, nz, seg, cols), BF16),
            pltpu.VMEM((chunks, nz, seg, cols), BF16),
            pltpu.VMEM((chunks, NY, 2 * half, cols), BF16),
            pltpu.VMEM((3, rows, flat), BF16),
            pltpu.VMEM((3, rows, flat), BF16),
            pltpu.VMEM((2, 2, half, flat), BF16),
            pltpu.VMEM((3, 2 * half, flat), F32),
        ]
        + [dma(shape) for shape in pairs for _ in range(2)],
        compiler_params=pltpu.CompilerParams(
            collective_id=0, has_side_effects=True, vmem_limit_bytes=46 << 20
        ),
        cost_estimate=pl.CostEstimate(
            flops=4 * nx * rows * flat * share_rows, bytes_accessed=8 << 20, transcendentals=0
        ),
    )(factors, send, meta, place)


def on_device(factors, amplitudes, block_list, owner_map):
    pair_count = lax.axis_size("pair")
    aux_count = lax.axis_size("aux")
    share = lax.axis_index("aux")
    block_count, block_width, _ = amplitudes.shape
    virt = factors.shape[2]
    lanes = max(128, virt * virt)
    part = block_width // aux_count
    ids = lax.iota(jnp.int32, block_count)
    hits = block_list[:, 0][:, None] == lax.iota(jnp.int32, owner_map.shape[0])[None, :]
    owners = jnp.sum(jnp.where(hits, owner_map[None, :], 0), axis=1)
    combo = block_list[:, 1] * virt + block_list[:, 2]
    same = (owners[:, None] == owners[None, :]) & (ids[None, :] < ids[:, None])
    rank = jnp.sum(same.astype(jnp.int32), axis=1)
    slots = owners * CAP + rank
    placing = (slots[:, None] == lax.iota(jnp.int32, pair_count * CAP)[None, :]).astype(BF16)
    at_combo = (combo[:, None] == lax.iota(jnp.int32, lanes)[None, :]).astype(BF16)
    meta = jnp.einsum("js,jn->sn", placing, at_combo, preferred_element_type=F32)
    mine = lax.dynamic_slice_in_dim(amplitudes, share * part, part, axis=1)
    sent = jnp.einsum("js,jm->sm", placing, mine.reshape(block_count, -1), preferred_element_type=F32)
    to_owner = owners[:, None] == lax.iota(jnp.int32, pair_count)[None, :]
    place = jnp.stack([to_owner & (rank == r)[:, None] for r in range(CAP)]).astype(BF16)
    return cycle(
        factors.reshape(-1, virt, block_width),
        sent.astype(BF16).reshape(pair_count, CAP, part, block_width),
        meta.reshape(pair_count, CAP, lanes),
        place,
    )


def solution(mesh):
    placed = (P("pair", "aux", None, None), P("pair", None, None), P("pair", None), P())
    return jax.shard_map(
        on_device, mesh=mesh, in_specs=placed, out_specs=P("pair", None, None), check_vma=False
    )
```

```python
import functools

import jax
import jax.numpy as jnp
from jax import lax
from jax.experimental import pallas as pl
from jax.experimental.pallas import tpu as pltpu
from jax.sharding import PartitionSpec as P

CAP = 2
ORDER = ((3, 0), (0, 0), (1, 0), (2, 0), (0, 1), (1, 1), (2, 1), (3, 1))
NY = 4
F32 = jnp.float32
BF16 = jnp.bfloat16
MESH = pl.DeviceIdType.MESH
NT = (((1,), (1,)), ((), ()))
TN = (((0,), (0,)), ((), ()))


def cycle_kernel(
    nz, nx, factor_ref, send_ref, meta_ref, place_ref, out_ref, f_ref, got_ref, picks_ref, bsend,
    bgot, w_ref, wall, sibtx, sibrx, part, ytx, yrx, ztx, zrx, zg, xt, ptx, prx,
    acc, s_m, r_m, s_a, r_a, s_b, r_b, s_j, r_j, s_w, r_w, s_sib, r_sib, s_y, r_y,
    s_z, r_z, s_gz, r_gz, s_gy, r_gy, s_gs, r_gs, s_p, r_p,
):
    pair, aux = lax.axis_index("pair"), lax.axis_index("aux")
    core, z, y = lax.rem(pair, 2), lax.rem(pair // 2, nz), pair // (2 * nz)
    half = sibtx.shape[2]
    seg = half // nz
    mid = half // 2
    cols = part.shape[3]
    rows = 2 * half
    chunks = len(ORDER)

    def at(y_, z_, c_):
        return {"pair": (lax.rem(y_ + NY, NY) * nz + lax.rem(z_ + nz, nz)) * 2 + c_}

    sib = at(y, z, 1 - core)
    up, down = at(y + 1, z, core), at(y - 1, z, core)
    right, left = {"aux": lax.rem(aux + 1, nx)}, {"aux": lax.rem(aux + nx - 1, nx)}
    across = {"aux": lax.rem(aux + 2, nx)}

    def copy(src, dst, send, recv, to):
        return pltpu.make_async_remote_copy(
            src_ref=src, dst_ref=dst, send_sem=send, recv_sem=recv, device_id=to, device_id_type=MESH
        )

    n = 2 * NY * nz
    barrier = pltpu.get_barrier_semaphore()
    for peer in (right, left, across):
        pl.semaphore_signal(barrier, inc=1, device_id=peer, device_id_type=MESH)

    def peer_at(d):
        return lax.rem(pair + d, n)

    def greet(d, carry):
        pl.semaphore_signal(
            barrier, inc=1, device_id={"pair": peer_at(d)}, device_id_type=MESH
        )
        return carry

    lax.fori_loop(1, n, greet, 0)
    pl.semaphore_wait(barrier, n + 2)

    sent = []

    def go(*args):
        c = copy(*args)
        c.start()
        sent.append(c)
        return c

    def landed(dst, recv):
        copy(dst, dst, recv, recv, sib).wait_recv()

    thin = send_ref.shape[2] // 2
    width = send_ref.shape[3]
    virt = w_ref.shape[1] // width

    def meta_copy(d):
        to = peer_at(d)
        return copy(
            meta_ref.at[to], picks_ref.at[pair], s_m.at[0], r_m.at[0], {"pair": to}
        )

    def out_copy(h, d):
        to = peer_at(d)
        return copy(
            send_ref.at[to, :, h * thin : (h + 1) * thin, :], got_ref.at[h, pair], s_a.at[h],
            r_a.at[h], {"pair": to},
        )

    def back_copy(h, d):
        to = peer_at(d)
        return copy(bsend.at[h, to], bgot.at[h, pair], s_b.at[h], r_b.at[h], {"pair": to})

    def each_peer(act):
        def one(d, carry):
            act(d)
            return carry

        lax.fori_loop(1, n, one, 0)

    def first(d):
        meta_copy(d).start()
        out_copy(0, d).start()

    each_peer(first)
    each_peer(lambda d: out_copy(1, d).start())
    picks_ref[pair] = meta_ref[pair]
    for h in range(2):
        got_ref[h, pair] = send_ref[pair, :, h * thin : (h + 1) * thin, :]
    step = 64 if f_ref.shape[0] % 64 == 0 else f_ref.shape[0]

    def flatten(i, carry):
        at_rows = pl.ds(pl.multiple_of(i * step, step), step)
        f_ref[at_rows, :] = factor_ref[at_rows].astype(F32).reshape(step, -1).astype(BF16)
        return carry

    lax.fori_loop(0, f_ref.shape[0] // step, flatten, 0)

    def combine(h):
        total = 0.0
        for r in range(CAP):
            rows_r = got_ref[h, :, r].astype(F32).reshape(n, thin * width).astype(BF16)
            total = total + lax.dot_general(
                picks_ref[:, r, :].astype(BF16), rows_r, TN, preferred_element_type=F32
            )
        total = total[: virt * virt].reshape(virt * virt, thin, width).astype(BF16)
        for a in range(virt):
            for c in range(virt):
                low = h * rows + a * thin
                w_ref[low : low + thin, c * width : (c + 1) * width] = total[a * virt + c]
        piece = slice(h * rows, (h + 1) * rows)
        go(w_ref.at[piece], wall.at[0, piece], s_w.at[h, 0], r_w.at[h, 0], right)
        go(w_ref.at[piece], wall.at[1, piece], s_w.at[h, 1], r_w.at[h, 1], left)

    landed(picks_ref.at[: n - 1], r_m.at[0])
    landed(got_ref.at[0, : n - 1], r_a.at[0])
    combine(0)

    own = pl.multiple_of(core * half, half)
    other = pl.multiple_of((1 - core) * half, half)

    def weights_product(t):
        share, h = ORDER[t]
        piece = slice(h * rows, (h + 1) * rows)
        low, high = slice(h * rows, h * rows + half), slice(h * rows + half, (h + 1) * rows)
        if share == 0:
            landed(wall.at[0, piece], r_w.at[h, 0])
            go(wall.at[0, low], wall.at[2, low], s_w.at[h, 2], r_w.at[h, 2], right)
            landed(wall.at[1, piece], r_w.at[h, 1])
            go(wall.at[1, high], wall.at[2, high], s_w.at[h, 3], r_w.at[h, 3], left)
        if share == 2:
            landed(wall.at[2, low], r_w.at[h, 2])
            landed(wall.at[2, high], r_w.at[h, 3])
        w = (w_ref if share == 3 else wall.at[share]).at[piece]
        w_both = jnp.concatenate([w[pl.ds(other, half), :], w[pl.ds(own, half), :]], axis=0)

        def block(b, carry):
            got = lax.dot_general(
                w_both, f_ref[pl.ds(pl.multiple_of(b * cols, cols), cols), :], NT,
                preferred_element_type=F32,
            )
            sibtx[t, b] = got[:half]
            part[t, b] = got[half:]
            return carry

        lax.fori_loop(0, NY, block, 0)
        go(sibtx.at[t], sibrx.at[t], s_sib.at[t], r_sib.at[t], sib)

    def core_sum(t):
        landed(sibrx.at[t], r_sib.at[t])

        def block(b, carry):
            part[t, b] = part[t, b] + sibrx[t, b]
            return carry

        lax.fori_loop(0, NY, block, 0)
        for d in (2, 1, 3):
            ytx[t, d] = part[t, lax.rem(y + d, NY)].astype(BF16)
            go(ytx.at[t, d], yrx.at[t, d], s_y.at[t, d], r_y.at[t, d], at(y + d, z, core))

    def z_copy(t, d):
        to = lax.rem(z + d, nz)
        return copy(ztx.at[t, to], zrx.at[t, d], s_z.at[t], r_z.at[t], at(y, z + d, core))

    def y_sum(t):
        total = part[t, y]
        for d in (1, 3, 2):
            landed(yrx.at[t, d], r_y.at[t, d])
            total = total + yrx[t, d].astype(F32)
        ztx[t] = total.reshape(nz, seg, cols).astype(BF16)

        def send(d, carry):
            z_copy(t, d).start()
            return carry

        lax.fori_loop(1, nz, send, 0)

    def g_copy(t, d):
        mine = zg.at[t, z]
        return copy(mine, mine, s_gz.at[t], r_gz.at[t], at(y, z + d, core))

    def z_sum(t):
        landed(zrx.at[t, 1:], r_z.at[t])

        def add(d, total):
            return total + zrx[t, d].astype(F32)

        total = lax.fori_loop(1, nz, add, ztx[t, z].astype(F32))
        zg[t, z] = total.astype(BF16)

        def send(d, carry):
            g_copy(t, d).start()
            return carry

        lax.fori_loop(1, nz, send, 0)

    def half_of(t, y_, start, size):
        first = pl.multiple_of(core * half + start, mid)
        return xt.at[t, lax.rem(y_ + NY, NY), pl.ds(first, size), :]

    def z_gather(t):
        landed(zrx.at[t, 1:], r_gz.at[t])
        joined = zg[t].astype(F32).reshape(half, cols).astype(BF16)
        xt[t, y, pl.ds(pl.multiple_of(core * half, half), half), :] = joined
        mine = half_of(t, y, 0, half)
        for d in (2, 1, 3):
            go(mine, mine, s_gy.at[t, d], r_gy.at[t, d], at(y + d, z, core))
        go(mine, mine, s_gs.at[t, 0], r_gs.at[t, 0], sib)

    def y_gather(t):
        for d in (1, 3, 2):
            piece = half_of(t, y - d, 0, half)
            landed(piece, r_gy.at[t, d])
            go(piece, piece, s_gs.at[t, d], r_gs.at[t, d], sib)

    def block_product(t):
        for k in range(4):
            landed(half_of(t, y, 0, half), r_gs.at[t, k])

        share, h = ORDER[t]
        piece = slice(h * rows, (h + 1) * rows)
        k = 1 + h if share == 3 else 0

        def block(b, carry):
            got = jnp.dot(
                xt[t, b], f_ref[pl.ds(pl.multiple_of(b * cols, cols), cols), :],
                preferred_element_type=F32,
            )
            acc[k] = jnp.where(b == 0, got, acc[k] + got)
            return carry

        lax.fori_loop(0, NY, block, 0)
        if share < 3:
            ptx[share, piece] = acc[0].astype(BF16)
        if share == 0:
            go(ptx.at[0, piece], prx.at[1, piece], s_p.at[h, 1], r_p.at[h, 1], left)
        if share == 1:
            go(ptx.at[1, piece], prx.at[0, piece], s_p.at[h, 0], r_p.at[h, 0], right)
        if share == 2:
            go(ptx.at[2, piece], prx.at[2, piece], s_p.at[h, 2], r_p.at[h, 2], across)

    stages = (
        weights_product, core_sum, y_sum, z_sum, z_gather, y_gather, block_product,
    )
    def give_back(h):
        piece = slice(h * rows, (h + 1) * rows)
        for k in range(3):
            landed(prx.at[k, piece], r_p.at[h, k])
        total = acc[1 + h]
        for source in range(3):
            total = total + prx[source, piece].astype(F32)
        blocks = [
            total[a * thin : (a + 1) * thin, c * width : (c + 1) * width][None]
            for a in range(virt)
            for c in range(virt)
        ]
        flat = jnp.concatenate(blocks, axis=0).reshape(virt * virt, thin * width).astype(BF16)
        for r in range(CAP):
            chosen = picks_ref[:, r, :][:, : virt * virt].astype(BF16)
            got = jnp.dot(chosen, flat, preferred_element_type=F32)
            bsend[h, :, r] = got.reshape(n, thin, width).astype(BF16)
        each_peer(lambda d: back_copy(h, d).start())
        bgot[h, pair] = bsend[h, pair]

    for step in range(len(stages) + chunks - 1):
        if step == 3:
            landed(got_ref.at[1, : n - 1], r_a.at[1])
            combine(1)
        if step == 12:
            give_back(0)
        for k in reversed(range(len(stages))):
            if 0 <= step - k < chunks:
                stages[k](step - k)
    give_back(1)

    count = out_ref.shape[0]

    def spot(who, h):
        low = lax.rem(who + nx, nx) * (2 * thin) + h * thin
        return out_ref.at[:, pl.ds(pl.multiple_of(low, thin), thin), :]

    for h in range(2):
        landed(bgot.at[h, : n - 1], r_b.at[h])
        total = 0.0
        for r in range(CAP):
            rows_r = bgot[h, :, r].astype(F32).reshape(n, thin * width).astype(BF16)
            total = total + jnp.dot(place_ref[r], rows_r, preferred_element_type=F32)
        low = pl.multiple_of(aux * (2 * thin) + h * thin, thin)
        out_ref[:, pl.ds(low, thin), :] = total.reshape(count, thin, width).astype(BF16)
        mine = spot(aux, h)
        for k, to in enumerate((across, right, left)):
            go(mine, mine, s_j.at[h, k], r_j.at[h, k], to)
    for h in range(2):
        for k, d in enumerate((2, -1, 1)):
            landed(spot(aux + d, h), r_j.at[h, k])

    def left_here(src, send):
        copy(src, src, send, send, sib).wait_send()

    left_here(picks_ref.at[: n - 1], s_m.at[0])
    for h in range(2):
        left_here(got_ref.at[h, : n - 1], s_a.at[h])
        left_here(bgot.at[h, : n - 1], s_b.at[h])
    for c in sent:
        c.wait_send()
    for t in range(chunks):
        left_here(zrx.at[t, 1:], s_z.at[t])
        left_here(zrx.at[t, 1:], s_gz.at[t])


def cycle(factors, send, meta, place):
    n, _, part, width = send.shape
    nx = lax.axis_size("aux")
    nz = n // (2 * NY)
    share_rows, virt, _ = factors.shape
    rows, flat = virt * part, virt * width
    half, cols = rows // 4, share_rows // NY
    chunks = len(ORDER)
    seg, mid, thin = half // nz, half // 2, part // 2
    dma = pltpu.SemaphoreType.DMA
    vmem = pl.BlockSpec(memory_space=pltpu.VMEM)
    pairs = [
        (1,), (2,), (2,), (2, 3), (2, 4), (chunks,), (chunks, NY), (chunks,), (chunks,),
        (chunks, 4), (chunks, 4), (2, 3),
    ]
    return pl.pallas_call(
        functools.partial(cycle_kernel, nz, nx),
        out_shape=jax.ShapeDtypeStruct((place.shape[1], nx * part, width), BF16),
        in_specs=[vmem] * 4,
        out_specs=vmem,
        scratch_shapes=[
            pltpu.VMEM((share_rows, flat), BF16),
            pltpu.VMEM((2, n, CAP, thin, width), BF16),
            pltpu.VMEM(meta.shape, F32),
            pltpu.VMEM((2, n, CAP, thin, width), BF16),
            pltpu.VMEM((2, n, CAP, thin, width), BF16),
            pltpu.VMEM((rows, flat), BF16),
            pltpu.VMEM((3, rows, flat), BF16),
            pltpu.VMEM((chunks, NY, half, cols), F32),
            pltpu.VMEM((chunks, NY, half, cols), F32),
            pltpu.VMEM((chunks, NY, half, cols), F32),
            pltpu.VMEM((chunks, NY, half, cols), BF16),
            pltpu.VMEM((chunks, NY, half, cols), BF16),
            pltpu.VMEM((chunks, nz, seg, cols), BF16),
            pltpu.VMEM((chunks, nz, seg, cols), BF16),
            pltpu.VMEM((chunks, nz, seg, cols), BF16),
            pltpu.VMEM((chunks, NY, 2 * half, cols), BF16),
            pltpu.VMEM((3, rows, flat), BF16),
            pltpu.VMEM((3, rows, flat), BF16),
            pltpu.VMEM((3, 2 * half, flat), F32),
        ]
        + [dma(shape) for shape in pairs for _ in range(2)],
        compiler_params=pltpu.CompilerParams(
            collective_id=0, has_side_effects=True, vmem_limit_bytes=46 << 20
        ),
        cost_estimate=pl.CostEstimate(
            flops=4 * nx * rows * flat * share_rows, bytes_accessed=8 << 20, transcendentals=0
        ),
    )(factors, send, meta, place)


def on_device(factors, amplitudes, block_list, owner_map):
    pair_count = lax.axis_size("pair")
    aux_count = lax.axis_size("aux")
    share = lax.axis_index("aux")
    block_count, block_width, _ = amplitudes.shape
    virt = factors.shape[2]
    lanes = max(128, virt * virt)
    part = block_width // aux_count
    ids = lax.iota(jnp.int32, block_count)
    hits = block_list[:, 0][:, None] == lax.iota(jnp.int32, owner_map.shape[0])[None, :]
    owners = jnp.sum(jnp.where(hits, owner_map[None, :], 0), axis=1)
    combo = block_list[:, 1] * virt + block_list[:, 2]
    same = (owners[:, None] == owners[None, :]) & (ids[None, :] < ids[:, None])
    rank = jnp.sum(same.astype(jnp.int32), axis=1)
    slots = owners * CAP + rank
    placing = (slots[:, None] == lax.iota(jnp.int32, pair_count * CAP)[None, :]).astype(BF16)
    at_combo = (combo[:, None] == lax.iota(jnp.int32, lanes)[None, :]).astype(BF16)
    meta = jnp.einsum("js,jn->sn", placing, at_combo, preferred_element_type=F32)
    mine = lax.dynamic_slice_in_dim(amplitudes, share * part, part, axis=1)
    sent = jnp.einsum("js,jm->sm", placing, mine.reshape(block_count, -1), preferred_element_type=F32)
    to_owner = owners[:, None] == lax.iota(jnp.int32, pair_count)[None, :]
    place = jnp.stack([to_owner & (rank == r)[:, None] for r in range(CAP)]).astype(BF16)
    return cycle(
        factors.reshape(-1, virt, block_width),
        sent.astype(BF16).reshape(pair_count, CAP, part, block_width),
        meta.reshape(pair_count, CAP, lanes),
        place,
    )


def solution(mesh):
    placed = (P("pair", "aux", None, None), P("pair", None, None), P("pair", None), P())
    return jax.shard_map(
        on_device, mesh=mesh, in_specs=placed, out_specs=P("pair", None, None), check_vma=False
    )
```
